32 devices in a mesh: row: 8 (over z, core), col: 4 (over y, x).
Axes of the slice: x: 2, y: 2, z: 4, core: 2. Of those that a mesh axis runs over, the one named last changes fastest.
Arguments:
- amplitudes: bfloat16 [16, 16, 800, 800], P('col', None, 'row'), as said below
- integrals: bfloat16 [16, 16, 800, 800], P('col', None, 'row'), may hold values from -6 to 6
- fock_virtual: bfloat16 [800, 800], replicated, may hold values from -0.21875 to 0.21875
- occ_levels: int32 [16], replicated, may hold values from -12 to -3
- vir_levels: int32 [800], replicated, may hold values from 2 to 21
- ladder_ints: bfloat16 [800, 800, 2, 800], P('row', 'col'), may hold values from -0.0078125 to 0.0078125
Outputs:
- new_amps: bfloat16 [16, 16, 800, 800], P('col', None, 'row')
- ladder: bfloat16 [16, 16, 2, 800], P('col', 'row')
The draws below stay inside these ranges and needn't reach their ends.
Inputs may be any that keep to these rules, and one draw needn't show every extreme that they name: amplitudes[i, j, a, b] equals amplitudes[j, i, b, a] exactly.
All inputs are finite; a program needn't handle non-finite values.
Results may differ from the reference program's by a relative error of at most 0.0049.
Values may be sent and summed in bfloat16 or wider, within the bound.
A program may use at most 384 MiB of HBM per device.

```python
import jax
import jax.numpy as jnp
from jax import lax

OCCUPIED = 16
VIRTUAL = 800
WINDOW = 2


def draw_amplitudes(key, part):
    sample = jax.random.normal(key, (OCCUPIED, OCCUPIED, VIRTUAL, VIRTUAL), jnp.float32)
    return ((sample + jnp.transpose(sample, (1, 0, 3, 2))) * 0.7071).astype(jnp.bfloat16)


def touch_ends(array, stream_key, low, top_value):
    place = [jax.random.randint(jax.random.fold_in(stream_key, axis), (), 0, length) for axis, length in enumerate(array.shape)]
    main_axis = array.shape.index(max(array.shape))
    beside = place[:main_axis] + [(place[main_axis] + 1) % array.shape[main_axis]] + place[main_axis + 1:]
    return array.at[tuple(place)].set(low).at[tuple(beside)].set(top_value)


def block_scale(rng, shape, cuts, least, top_value):
    level = 1.0
    for position, parts in cuts:
        heights = jax.random.uniform(jax.random.fold_in(jax.random.fold_in(rng, 6), position), (parts,), jnp.float32, least / len(cuts), top_value / len(cuts))
        level = level * jnp.repeat(jnp.exp(heights), shape[position] // parts).reshape((-1,) + (1,) * (len(shape) - 1 - position))
    return level


def normal_values(stream_key, dims, spread, bound, pieces=(), held_as=jnp.bfloat16):
    entries = jax.random.normal(stream_key, dims, jnp.float32) * spread
    if len(pieces) > 0:
        entries = block_scale(stream_key, dims, pieces, -0.22, 0.18) * entries
    return jnp.clip(entries, min=-bound, max=bound).astype(held_as)


def setup_inputs(seed: int = 0) -> dict:
    streams_of = jax.random.split(jax.random.key(seed), 7)
    return {
        "amplitudes": draw_amplitudes(jax.random.fold_in(streams_of[6], 71), 0),
        "integrals": normal_values(streams_of[1], (OCCUPIED, OCCUPIED, VIRTUAL, VIRTUAL), 1.0, 6.0, ((0, 4), (2, 8))),
        "fock_virtual": normal_values(streams_of[2], (VIRTUAL, VIRTUAL), VIRTUAL ** -0.5, 0.21875),
        "occ_levels": touch_ends(jax.random.randint(streams_of[3], (OCCUPIED,), -12, -2), jax.random.fold_in(streams_of[3], 1), -12, (-2) - 1).astype(jnp.int32),
        "vir_levels": touch_ends(jax.random.randint(streams_of[4], (VIRTUAL,), 2, 22), jax.random.fold_in(streams_of[4], 1), 2, 21).astype(jnp.int32),
        "ladder_ints": normal_values(streams_of[5], (VIRTUAL, VIRTUAL, WINDOW, VIRTUAL), (VIRTUAL * VIRTUAL) ** -0.5, 0.0078125, ((0, 8), (1, 4))),
    }


level_step = 0.1


def reference(amplitudes, integrals, fock_virtual, occ_levels, vir_levels, ladder_ints):
    amp_float = amplitudes.astype(jnp.float32)
    fock_float = fock_virtual.astype(jnp.float32)
    left_term = jnp.einsum('ac,ijcb->ijab', fock_float, amp_float)
    right_term = jnp.einsum('ijac,bc->ijab', amp_float, fock_float)
    dressed = integrals.astype(jnp.float32) + left_term + right_term
    summed = dressed + jnp.transpose(dressed, (1, 0, 3, 2))
    level_sum = vir_levels[None, None, :, None] + vir_levels[None, None, None, :] - occ_levels[:, None, None, None] - occ_levels[None, :, None, None]
    denom = level_sum.astype(jnp.float32) * level_step
    new_amps = (summed / denom).astype(jnp.bfloat16)
    flat_amps = jnp.moveaxis(new_amps.reshape(OCCUPIED * OCCUPIED, VIRTUAL, VIRTUAL), 1, 0)

    def accumulate(running, inputs):
        amp_rows, integral_rows = inputs
        weights = integral_rows.reshape(VIRTUAL, WINDOW * VIRTUAL)
        return running + jnp.dot(amp_rows, weights, preferred_element_type=jnp.float32), None

    initial = jnp.zeros((OCCUPIED * OCCUPIED, WINDOW * VIRTUAL), jnp.float32)
    running, unused = lax.scan(accumulate, initial, (flat_amps, ladder_ints))
    ladder = running.reshape(OCCUPIED, OCCUPIED, WINDOW, VIRTUAL).astype(jnp.bfloat16)
    return new_amps, ladder
```

```python
import functools

import jax
import jax.numpy as jnp
from jax import lax
from jax.experimental import pallas as pl
from jax.experimental.pallas import tpu as pltpu
from jax.sharding import PartitionSpec as P

level_step = 0.1
MESH = pl.DeviceIdType.MESH
LANES = 128
CHUNK = 8
AHEAD = 2
F32 = jnp.float32
BF16 = jnp.bfloat16
NT = (((1,), (1,)), ((), ()))


def up(n, m=LANES):
    return -(-n // m) * m


def partner(k, rows, cols, row, col):
    turn = k // cols
    away = rows // 2 + ((turn + 1) // 2) * (1 - 2 * (turn % 2))
    return ((row + away + rows) % rows, (col + k % cols + 1) % cols)


def greet_all(rows, cols, row, col):
    barrier = pltpu.get_barrier_semaphore()
    count = rows * cols

    def greet(k, carry):
        pl.semaphore_signal(
            barrier, inc=1, device_id=partner(k, rows, cols, row, col), device_id_type=MESH
        )
        return carry

    lax.fori_loop(0, count - 1, greet, 0)
    pl.semaphore_wait(barrier, count - 1)


def exchange_kernel(rows, cols, src, dst, send_sem, recv_sem, local_sem):
    count = rows * cols
    row, col = lax.axis_index("row"), lax.axis_index("col")
    me = row * cols + col
    greet_all(rows, cols, row, col)

    def copy_to(k):
        peer_row, peer_col = partner(k, rows, cols, row, col)
        return pltpu.make_async_remote_copy(
            src_ref=src.at[peer_row * cols + peer_col],
            dst_ref=dst.at[me],
            send_sem=send_sem.at[k],
            recv_sem=recv_sem.at[k],
            device_id=(peer_row, peer_col),
            device_id_type=MESH,
        )

    def begin(k, carry):
        copy_to(k).start()
        return carry

    def finish(k, carry):
        copy_to(k).wait()
        return carry

    lax.fori_loop(0, count - 1, begin, 0)
    own = pltpu.make_async_copy(src.at[me], dst.at[me], local_sem)
    own.start()
    lax.fori_loop(0, count - 1, finish, 0)
    own.wait()


def exchange(blocks, rows, cols, number):
    count = rows * cols
    return pl.pallas_call(
        functools.partial(exchange_kernel, rows, cols),
        out_shape=jax.ShapeDtypeStruct(blocks.shape, blocks.dtype),
        in_specs=[pl.BlockSpec(memory_space=pl.ANY)],
        out_specs=pl.BlockSpec(memory_space=pl.ANY),
        scratch_shapes=[
            pltpu.SemaphoreType.DMA((count - 1,)),
            pltpu.SemaphoreType.DMA((count - 1,)),
            pltpu.SemaphoreType.DMA,
        ],
        compiler_params=pltpu.CompilerParams(collective_id=number, has_side_effects=True),
    )(blocks)


def wire_shape(elements):
    lanes = 128
    while elements % lanes:
        lanes //= 2
    return (elements // lanes, lanes)


def turn_kernel(g, amps_ref, ints_ref, fock_ref, pick_ref, order_ref, out_ref, fock_rows):
    step = pl.program_id(0)
    for f in range(g.o):

        @pl.when(step == f)
        def _():
            start = f * g.o * g.v
            phase, tile = start % LANES, start // LANES
            width = up(phase + g.o * g.v)
            if f == 0:
                out_ref[...] = jnp.zeros_like(out_ref)
                fock_rows[...] = (
                    2.0 * jnp.dot(pick_ref[...], fock_ref[...], preferred_element_type=F32)
                ).astype(BF16)

            def part(m, carry):
                at = pl.ds(pl.multiple_of(m * g.turn_rows, 16), g.turn_rows)
                turned = lax.dot_general(
                    fock_rows[at, :], amps_ref[0], NT, preferred_element_type=F32
                ) + lax.dot_general(pick_ref[at, :], ints_ref[0], NT, preferred_element_type=F32)
                ordered = jnp.dot(
                    turned.astype(BF16), order_ref[...], preferred_element_type=F32
                )
                for q in range(g.cols):
                    piece = ordered[:, q * g.order_width : (q + 1) * g.order_width]
                    if phase:
                        piece = pltpu.roll(piece, phase, 1)
                    lanes = pl.ds(tile * LANES, width)
                    out_ref[q, at, lanes] += piece[:, :width].astype(BF16)
                return carry

            lax.fori_loop(0, g.turn_total // g.turn_rows, part, 0)


class Sizes:
    pass


def sizes(rows, cols, amplitudes, ladder_ints):
    g = Sizes()
    g.rows, g.cols = rows, cols
    g.o, g.O, g.v, g.V = amplitudes.shape
    g.window = ladder_ints.shape[2]
    g.d = ladder_ints.shape[1]
    g.a = CHUNK
    g.k = -(-g.v // g.a)
    g.wire = up(g.o * g.o * g.v)
    g.pair = g.o * g.O
    g.nk = g.a * g.d
    g.nkp = up(g.nk)
    g.turn_total = g.k * rows * g.a
    g.turn_rows = max(t for t in range(16, 449, 16) if g.turn_total % t == 0)
    phases = [(f * g.o * g.v) % LANES for f in range(g.o)]
    g.order_width = up(g.o * g.v + max(phases))
    g.wide = up(g.V, 256)
    g.split_rows = max(t for t in range(16, 401, 16) if g.nk % t == 0)
    return g


def turned_blocks(g, amps, ints, fock_virtual):
    r = jnp.arange(g.turn_total)
    k, dest, a = r // (g.rows * g.a), (r // g.a) % g.rows, r % g.a
    wanted = dest * g.v + jnp.minimum(k * g.a, g.v - g.a) + a
    pick = (wanted[:, None] == jnp.arange(g.V)[None, :]).astype(BF16)
    source = jnp.arange(g.v * g.O)
    u, s = source // g.O, source % g.O
    goes = (s // g.o) * g.order_width + (s % g.o) * g.v + u
    order = (goes[:, None] == jnp.arange(g.cols * g.order_width)[None, :]).astype(BF16)
    whole = lambda shape: pl.BlockSpec(shape, lambda f: (0,) * len(shape), pipeline_mode=pl.Buffered(1))
    return pl.pallas_call(
        functools.partial(turn_kernel, g),
        grid=(g.o,),
        in_specs=[
            pl.BlockSpec((1, g.v * g.O, g.V), lambda f: (f, 0, 0)),
            pl.BlockSpec((1, g.v * g.O, g.V), lambda f: (f, 0, 0)),
            whole(fock_virtual.shape),
            whole(pick.shape),
            whole(order.shape),
        ],
        out_specs=whole((g.cols, g.turn_total, g.wire)),
        out_shape=jax.ShapeDtypeStruct((g.cols, g.turn_total, g.wire), BF16),
        scratch_shapes=[pltpu.VMEM((g.turn_total, g.V), BF16)],
        compiler_params=pltpu.CompilerParams(vmem_limit_bytes=60 * 2**20),
    )(amps, ints, fock_virtual, pick, order)


def main_kernel(
    g,
    wire_ref, amps_ref, ints_ref, slab_ref, fock_ref, place_ref, base_ref, occ_ref, vir_ref,
    out_ref, term_ref,
    got, sent_on, came, amp_buf, int_buf, slab_buf, split_buf, mirror, mirror_low, total, line, result,
    x_send, x_recv, n_send, n_recv, in_sem, slab_sem, out_sem,
):
    rows, cols = g.rows, g.cols
    count = rows * cols
    row, col = lax.axis_index("row"), lax.axis_index("col")
    block_rows = g.a * g.O

    def first(k):
        return jnp.minimum(k * g.a, g.v - g.a)

    def send_blocks(k):
        def begin(t, carry):
            peer_row, peer_col = partner(t, rows, cols, row, col)
            at = pl.multiple_of((k * rows + peer_row) * g.a, g.a)
            pltpu.make_async_remote_copy(
                src_ref=wire_ref.at[peer_col, pl.ds(at, g.a), :],
                dst_ref=got.at[k, col * rows + row],
                send_sem=x_send.at[k],
                recv_sem=x_recv.at[k],
                device_id=(peer_row, peer_col),
                device_id_type=MESH,
            ).start()
            return carry

        lax.fori_loop(0, count - 1, begin, 0)
        at = pl.multiple_of((k * rows + row) * g.a, g.a)
        pltpu.make_async_copy(
            wire_ref.at[col, pl.ds(at, g.a), :], got.at[k, col * rows + row], x_recv.at[k]
        ).start()

    def loads(k, slot):
        at = pl.ds(pl.multiple_of(first(k) * g.O, g.O), block_rows)
        return (
            pltpu.make_async_copy(amps_ref.at[:, at, :], amp_buf.at[slot], in_sem.at[0, slot]),
            pltpu.make_async_copy(ints_ref.at[:, at, :], int_buf.at[slot], in_sem.at[1, slot]),
        )

    def slab_load(k, slot):
        return pltpu.make_async_copy(
            slab_ref.at[pl.ds(first(k) * g.d, g.nk)], slab_buf.at[slot], slab_sem.at[slot]
        )

    def out_store(k, slot):
        at = pl.ds(pl.multiple_of(first(k) * g.O, g.O), block_rows)
        return pltpu.make_async_copy(result.at[slot], out_ref.at[:, at, :], out_sem.at[slot])

    def send_amps(k, slot):
        for n in range(1, cols):
            peer = (col + n) % cols
            pltpu.make_async_remote_copy(
                src_ref=sent_on.at[slot, peer],
                dst_ref=came.at[k, col],
                send_sem=n_send.at[k],
                recv_sem=n_recv.at[k],
                device_id=(row, peer),
                device_id_type=MESH,
            ).start()
        pltpu.make_async_copy(sent_on.at[slot, col], came.at[k, col], n_recv.at[k]).start()

    def all_sent(k, slot):
        part = sent_on.at[slot, pl.ds(0, cols - 1)]
        pltpu.make_async_copy(part, part, n_send.at[k]).wait()

    def combine(k, slot):
        def spread(t, carry):
            at = (t // rows) * g.o
            block = got[k, t].astype(F32)
            for f in range(g.o):
                for s in range(g.o):
                    start = (f * g.o + s) * g.v
                    tile, phase = start // LANES, start % LANES
                    span = min(tile * LANES + up(phase + g.v), g.wire) - tile * LANES
                    piece = block[:, tile * LANES : tile * LANES + span]
                    if phase:
                        piece = pltpu.roll(piece, span - phase, 1)
                    goal = pl.ds(s * block_rows + at + f, g.a, stride=g.O)
                    mirror[t % rows, goal, :] = piece[:, :LANES]
            return carry

        lax.fori_loop(0, count, spread, 0)
        for n in range(rows):
            mirror_low[:, n * LANES : (n + 1) * LANES] = mirror[n].astype(BF16)
        mine = amp_buf[slot].reshape(g.o * block_rows, g.V)

        def column(n, carry):
            lane = pl.ds(pl.multiple_of(n * 256, 256), 256)
            total[:, lane] = jnp.dot(
                mirror_low[...], place_ref[:, lane], preferred_element_type=F32
            ) + jnp.dot(mine, fock_ref[:, lane], preferred_element_type=F32)
            return carry

        lax.fori_loop(0, g.wide // 256, column, 0)
        start = first(k)
        lane_of = lax.broadcasted_iota(jnp.int32, (g.pair, LANES), 1)
        for a in range(g.a):
            level = vir_ref[row * g.v + start + a]
            fresh = start + a >= k * g.a
            for i in range(g.o):
                at = i * block_rows + a * g.O
                summed = total[at : at + g.O, : g.V] + int_buf[
                    slot, i, a * g.O : (a + 1) * g.O, :
                ].astype(F32)
                levels = base_ref[...] + (level - occ_ref[col * g.o + i])
                value = summed / (levels.astype(F32) * level_step)
                result[slot, i, a * g.O : (a + 1) * g.O, :] = value.astype(BF16)
                line[i * g.O : (i + 1) * g.O, : g.V] = jnp.where(fresh, value, 0.0)
            goal = a * g.d
            goal_tile, goal_phase = goal // LANES, goal % LANES
            goal_tiles = up(goal_phase + g.d) // LANES
            for q in range(cols):
                begin, end = q * g.d, (q + 1) * g.d
                tiles = max(goal_tiles, -(-end // LANES) - begin // LANES)
                left = min(begin // LANES, g.wide // LANES - tiles)
                piece = line[:, left * LANES : (left + tiles) * LANES]
                shift = (goal_phase - (begin - left * LANES)) % (tiles * LANES)
                if shift:
                    piece = pltpu.roll(piece, shift, 1)
                for t in range(goal_tiles):
                    lane = slice((goal_tile + t) * LANES, (goal_tile + t + 1) * LANES)
                    new = piece[:, t * LANES : (t + 1) * LANES]
                    if t == 0 and goal_phase:
                        old = sent_on[slot, q, :, lane].astype(F32)
                        new = jnp.where(lane_of >= goal_phase, new, old)
                    if a == g.a - 1 and t == goal_tiles - 1 and g.nkp > g.nk:
                        new = jnp.where(lane_of < g.nk - (goal_tile + t) * LANES, new, 0.0)
                    sent_on[slot, q, :, lane] = new.astype(BF16)

    def multiply(k, slot):
        pltpu.make_async_copy(came.at[k], came.at[k], n_recv.at[k]).wait()
        slab_load(k, slot).wait()

        def split(m, carry):
            at = pl.ds(pl.multiple_of(m * g.split_rows, 16), g.split_rows)
            parted = pltpu.einshape("tab->atb", slab_buf[slot, at])
            for w in range(g.window):
                split_buf[w, at, :] = parted[w]
            return carry

        lax.fori_loop(0, g.nk // g.split_rows, split, 0)

        left = came[k].reshape(cols * g.pair, g.nkp)[:, : g.nk]

        def column(w, carry):
            term_ref[w] += jnp.dot(left, split_buf[w], preferred_element_type=F32)
            return carry

        lax.fori_loop(0, g.window, column, 0)

    greet_all(rows, cols, row, col)
    for k in range(min(AHEAD, g.k)):
        send_blocks(k)
    for copy in loads(0, 0):
        copy.start()
    for k in range(min(2, g.k)):
        slab_load(k, k).start()
    term_ref[...] = jnp.zeros_like(term_ref)
    line[...] = jnp.zeros_like(line)

    def chunk(k, carry):
        slot = k % 2

        @pl.when(k + AHEAD < g.k)
        def _():
            send_blocks(k + AHEAD)

        @pl.when(k + 1 < g.k)
        def _():
            for copy in loads(k + 1, (k + 1) % 2):
                copy.start()

        for copy in loads(k, slot):
            copy.wait()
        pltpu.make_async_copy(got.at[k], got.at[k], x_recv.at[k]).wait()

        @pl.when(k >= 2)
        def _():
            all_sent(k - 2, slot)

        combine(k, slot)
        send_amps(k, slot)

        @pl.when(k >= 1)
        def _():
            out_store(k - 1, (k + 1) % 2).wait()

        out_store(k, slot).start()

        @pl.when(k >= 1)
        def _():
            multiply(k - 1, (k + 1) % 2)

            @pl.when(k + 1 < g.k)
            def _():
                slab_load(k + 1, (k + 1) % 2).start()

        return carry

    lax.fori_loop(0, g.k, chunk, 0)
    multiply(g.k - 1, (g.k - 1) % 2)
    for k in range(max(0, g.k - 2), g.k):
        all_sent(k, k % 2)
    out_store(g.k - 1, (g.k - 1) % 2).wait()

    def drain(k, carry):
        part = got.at[k, pl.ds(0, count - 1)]
        pltpu.make_async_copy(part, part, x_send.at[k]).wait()
        return carry

    lax.fori_loop(0, g.k, drain, 0)


def main_call(g, wire, amps, ints, slab, fock_virtual, occ_levels, vir_levels):
    b = jnp.arange(g.wide)
    lane = jnp.arange(g.rows * LANES)
    where = jnp.where(lane % LANES < g.v, (lane // LANES) * g.v + lane % LANES, -1)
    place = (where[:, None] == b[None, :]).astype(BF16)
    fock = jnp.pad(jnp.transpose(fock_virtual * 2), ((0, 0), (0, g.wide - g.V)))
    base = vir_levels[None, :] - occ_levels[:, None]
    count = g.rows * g.cols
    block_rows = g.a * g.O
    any_space = pl.BlockSpec(memory_space=pl.ANY)
    vmem = pl.BlockSpec(memory_space=pltpu.VMEM)
    smem = pl.BlockSpec(memory_space=pltpu.SMEM)
    dma = pltpu.SemaphoreType.DMA
    return pl.pallas_call(
        functools.partial(main_kernel, g),
        out_shape=(
            jax.ShapeDtypeStruct((g.o, g.v * g.O, g.V), BF16),
            jax.ShapeDtypeStruct((g.window, g.cols * g.pair, g.V), F32),
        ),
        in_specs=[any_space] * 4 + [vmem] * 3 + [smem] * 2,
        out_specs=(any_space, vmem),
        scratch_shapes=[
            pltpu.VMEM((g.k, count, g.a, g.wire), BF16),
            pltpu.VMEM((2, g.cols, g.pair, g.nkp), BF16),
            pltpu.VMEM((g.k, g.cols, g.pair, g.nkp), BF16),
            pltpu.VMEM((2, g.o, block_rows, g.V), BF16),
            pltpu.VMEM((2, g.o, block_rows, g.V), BF16),
            pltpu.VMEM((2, g.nk, g.window, g.V), BF16),
            pltpu.VMEM((g.window, g.nk, g.V), BF16),
            pltpu.VMEM((g.rows, g.o * block_rows, LANES), F32),
            pltpu.VMEM((g.o * block_rows, g.rows * LANES), BF16),
            pltpu.VMEM((g.o * block_rows, g.wide), F32),
            pltpu.VMEM((g.pair, g.wide), F32),
            pltpu.VMEM((2, g.o, block_rows, g.V), BF16),
            dma((g.k,)), dma((g.k,)), dma((g.k,)), dma((g.k,)),
            dma((2, 2)), dma((2,)), dma((2,)),
        ],
        compiler_params=pltpu.CompilerParams(
            collective_id=0, has_side_effects=True, vmem_limit_bytes=66_000_000
        ),
    )(wire, amps, ints, slab, fock, place, base, occ_levels, vir_levels)


def body(rows, cols, amplitudes, integrals, fock_virtual, occ_levels, vir_levels, ladder_ints):
    g = sizes(rows, cols, amplitudes, ladder_ints)
    amps = jnp.transpose(amplitudes, (0, 2, 1, 3)).reshape(g.o, g.v * g.O, g.V)
    ints = jnp.transpose(integrals, (0, 2, 1, 3)).reshape(g.o, g.v * g.O, g.V)
    wire = turned_blocks(g, amps, ints, fock_virtual)
    slab = ladder_ints.reshape(g.v * g.d, g.window, g.V)
    result, term = main_call(g, wire, amps, ints, slab, fock_virtual, occ_levels, vir_levels)
    new_amps = jnp.transpose(result.reshape(g.o, g.v, g.O, g.V), (0, 2, 1, 3))
    occ_row = g.O // rows
    term = term.reshape(g.window, cols, g.o, rows, occ_row, g.V)
    term = jnp.transpose(term, (3, 1, 2, 4, 0, 5))
    elements = term.size // (rows * cols)
    blocks = term.astype(BF16).reshape((rows * cols,) + wire_shape(elements))
    parts = exchange(blocks, rows, cols, 1)
    ladder = jnp.sum(parts.astype(F32), axis=0).reshape(g.o, occ_row, g.window, g.V)
    return (new_amps, ladder.astype(BF16))


def solution(mesh):
    placed = (
        P("col", None, "row", None),
        P("col", None, "row", None),
        P(),
        P(),
        P(),
        P("row", "col", None, None),
    )
    return jax.shard_map(
        functools.partial(body, mesh.shape["row"], mesh.shape["col"]),
        mesh=mesh,
        in_specs=placed,
        out_specs=(P("col", None, "row", None), P("col", "row", None, None)),
        check_vma=False,
    )
```

```python
import functools

import jax
import jax.numpy as jnp
from jax import lax
from jax.experimental import pallas as pl
from jax.experimental.pallas import tpu as pltpu
from jax.sharding import PartitionSpec as P

level_step = 0.1
MESH = pl.DeviceIdType.MESH
LANES = 128
CHUNK = 8
AHEAD = 4
GROUPS = (2, 5, 6)
F32 = jnp.float32
BF16 = jnp.bfloat16
NT = (((1,), (1,)), ((), ()))


def up(n, m=LANES):
    return -(-n // m) * m


def partner(k, rows, cols, row, col):
    turn = k // cols
    away = rows // 2 + ((turn + 1) // 2) * (1 - 2 * (turn % 2))
    return ((row + away + rows) % rows, (col + k % cols + 1) % cols)


def greet_all(rows, cols, row, col):
    barrier = pltpu.get_barrier_semaphore()
    count = rows * cols

    def greet(k, carry):
        pl.semaphore_signal(
            barrier, inc=1, device_id=partner(k, rows, cols, row, col), device_id_type=MESH
        )
        return carry

    lax.fori_loop(0, count - 1, greet, 0)
    pl.semaphore_wait(barrier, count - 1)


class Sizes:
    pass


def sizes(rows, cols, amplitudes, ladder_ints):
    g = Sizes()
    g.rows, g.cols = rows, cols
    g.o, g.O, g.v, g.V = amplitudes.shape
    g.window = ladder_ints.shape[2]
    g.d = ladder_ints.shape[1]
    g.a = CHUNK
    g.k = -(-g.v // g.a)
    g.wire = up(g.o * g.o * g.v)
    g.pair = g.o * g.O
    g.nk = g.a * g.d
    g.nkp = up(g.nk)
    g.turn_total = g.k * rows * g.a
    starts = [f * g.o * g.v for f in range(g.o)]
    g.order_width = up(g.o * g.v + max(start % LANES for start in starts))
    g.wire = max([g.wire] + [start // LANES * LANES + g.order_width for start in starts])
    g.groups = []
    while sum(g.groups) < g.k:
        want = GROUPS[min(len(g.groups), len(GROUPS) - 1)]
        g.groups.append(min(want, g.k - sum(g.groups)))
    g.left = g.v - (g.k - 1) * g.a
    g.pack = 2 * g.left == g.a
    g.half = up(g.wire // 2)
    g.last = g.half if g.pack else g.wire
    g.each = g.O // rows * g.o
    g.wide = up(g.V, 256)
    g.split_rows = max(t for t in range(16, 401, 16) if g.nk % t == 0)
    return g


def main_kernel(
    g,
    amps_ref, ints_ref, slab_ref, raw_ref, occ_col_ref, vir_row_ref, occ_ref, vir_ref,
    out_ref, wire_ref, ladder_ref,
    got, came, came_col, came_row,
    x_send, x_recv, n_send, n_recv, in_sem, slab_sem, out_sem, turn_sem, wire_sem, end_sem,
):
    rows, cols = g.rows, g.cols
    count = rows * cols
    row, col = lax.axis_index("row"), lax.axis_index("col")
    block_rows = g.a * g.O

    def first(k):
        return jnp.minimum(k * g.a, g.v - g.a)

    def send_blocks(k, width):
        lanes = pl.ds(0, width)

        def begin(t, carry):
            peer_row, peer_col = partner(t, rows, cols, row, col)
            at = pl.multiple_of((k * rows + peer_row) * g.a, g.a)
            pltpu.make_async_remote_copy(
                src_ref=wire_ref.at[peer_col, pl.ds(at, g.a), lanes],
                dst_ref=got.at[k, col * rows + row, :, lanes],
                send_sem=x_send.at[k],
                recv_sem=x_recv.at[k],
                device_id=(peer_row, peer_col),
                device_id_type=MESH,
            ).start()
            return carry

        lax.fori_loop(0, count - 1, begin, 0)
        at = pl.multiple_of((k * rows + row) * g.a, g.a)
        pltpu.make_async_copy(
            wire_ref.at[col, pl.ds(at, g.a), lanes],
            got.at[k, col * rows + row, :, lanes],
            x_recv.at[k],
        ).start()

    def arrived(k, width):
        part = got.at[k, :, :, pl.ds(0, width)]
        pltpu.make_async_copy(part, part, x_recv.at[k]).wait()

    def gone(k, width):
        part = got.at[k, pl.ds(0, count - 1), :, pl.ds(0, width)]
        pltpu.make_async_copy(part, part, x_send.at[k]).wait()

    def turn(order, pick, fock_rows, amp_whole, int_whole, staged):
        def whole(step):
            f, slot = step % g.o, step % 2
            return (
                pltpu.make_async_copy(amps_ref.at[f], amp_whole.at[slot], turn_sem.at[0, slot]),
                pltpu.make_async_copy(ints_ref.at[f], int_whole.at[slot], turn_sem.at[1, slot]),
            )

        steps = len(g.groups) * g.o
        for copy in whole(0):
            copy.start()
        width = cols * g.order_width
        spin = lax.broadcasted_iota(jnp.int32, (g.O, width), 0)
        lane = lax.broadcasted_iota(jnp.int32, (g.O, width), 1)
        offset = lane - (spin // g.o) * g.order_width - (spin % g.o) * g.v

        def order_row(u, carry):
            at = pl.ds(pl.multiple_of(u * g.O, g.O), g.O)
            order[at, :] = jnp.where(offset == u, 1.0, 0.0).astype(BF16)
            return carry

        lax.fori_loop(0, g.v, order_row, 0)
        both = lax.broadcasted_iota(jnp.int32, (2 * g.a, g.V), 0)
        place_of = lax.broadcasted_iota(jnp.int32, (2 * g.a, g.V), 1)
        upper = jnp.where(both >= g.a, 1, 0)
        part = both - upper * g.a
        again = jnp.where(part < g.a - g.left, part + g.left, part) if g.pack else part

        def pick_rows(k, shape):
            def one(n, carry):
                at = pl.ds(pl.multiple_of((k * rows + 2 * n) * g.a, 2 * g.a), 2 * g.a)
                same = place_of - shape - upper * g.v == 2 * n * g.v + first(k)
                pick[at, :] = jnp.where(same, 1.0, 0.0).astype(BF16)
                return carry

            lax.fori_loop(0, rows // 2, one, 0)

        def pick_chunk(k, carry):
            pick_rows(k, part)
            return carry

        lax.fori_loop(0, g.k - 1, pick_chunk, 0)
        pick_rows(g.k - 1, again)
        greet_all(rows, cols, row, col)
        done = 0
        for number, size in enumerate(g.groups):
            height = size * rows * g.a
            at = slice(done * rows * g.a, done * rows * g.a + height)
            staged[:, :height] = jnp.zeros((cols, height, g.wire), BF16)
            fock_rows[:height] = (
                2.0 * jnp.dot(pick[at, :], raw_ref[...], preferred_element_type=F32)
            ).astype(BF16)

            def one(f, carry):
                step = number * g.o + f
                slot = step % 2

                @pl.when(step + 1 < steps)
                def _():
                    for copy in whole(step + 1):
                        copy.start()

                for copy in whole(step):
                    copy.wait()
                turned = lax.dot_general(
                    fock_rows[:height], amp_whole[slot], NT, preferred_element_type=F32
                ) + lax.dot_general(pick[at, :], int_whole[slot], NT, preferred_element_type=F32)
                turned = turned.astype(BF16)
                start = f * (g.o * g.v)
                lanes = pl.ds(pl.multiple_of(start // LANES * LANES, LANES), g.order_width)
                for q in range(cols):
                    piece = jnp.dot(
                        turned,
                        order[:, q * g.order_width : (q + 1) * g.order_width],
                        preferred_element_type=F32,
                    )
                    piece = pltpu.roll(piece, start % LANES, 1)
                    staged[q, :height, lanes] += piece.astype(BF16)
                return carry

            lax.fori_loop(0, g.o, one, 0)
            if g.pack and done + size == g.k:
                over = g.wire - g.half
                tail = slice(height - rows * g.a, height)
                high = lax.broadcasted_iota(jnp.int32, (rows * g.a, over), 0) % g.a < g.a - g.left
                for q in range(cols):
                    staged[q, tail, :over] = jnp.where(
                        high,
                        staged[q, tail, g.half :].astype(F32),
                        staged[q, tail, :over].astype(F32),
                    ).astype(BF16)
            copy = pltpu.make_async_copy(staged.at[:, pl.ds(0, height)], wire_ref.at[:, at], wire_sem)
            copy.start()
            copy.wait()
            for k in range(done, min(done + size, AHEAD)):
                send_blocks(k, g.last if k == g.k - 1 else g.wire)
            done += size

    def rest(
        sent_on, amp_buf, int_buf, slab_buf, split_buf, mirror, mirror_low, total, line, result,
        term_ref, fock_ref, place_ref, base_ref, send_col, send_row,
    ):
        def loads(k, slot):
            at = pl.ds(pl.multiple_of(first(k) * g.O, g.O), block_rows)
            return (
                pltpu.make_async_copy(amps_ref.at[:, at, :], amp_buf.at[slot], in_sem.at[0, slot]),
                pltpu.make_async_copy(ints_ref.at[:, at, :], int_buf.at[slot], in_sem.at[1, slot]),
            )

        def slab_load(k, slot):
            return pltpu.make_async_copy(
                slab_ref.at[pl.ds(first(k) * g.d, g.nk)], slab_buf.at[slot], slab_sem.at[slot]
            )

        def out_store(k, slot):
            at = pl.ds(pl.multiple_of(first(k) * g.O, g.O), block_rows)
            return pltpu.make_async_copy(result.at[slot], out_ref.at[:, at, :], out_sem.at[slot])

        def last_store():
            height = g.left * g.O
            slot = (g.k - 1) % 2
            return pltpu.make_async_copy(
                result.at[slot, :, pl.ds(block_rows - height, height), :],
                out_ref.at[:, pl.ds((g.k - 1) * g.a * g.O, height), :],
                out_sem.at[slot],
            )

        def send_amps(k, slot):
            for n in range(1, cols):
                peer = (col + n) % cols
                pltpu.make_async_remote_copy(
                    src_ref=sent_on.at[slot, peer],
                    dst_ref=came.at[k, col],
                    send_sem=n_send.at[k],
                    recv_sem=n_recv.at[k],
                    device_id=(row, peer),
                    device_id_type=MESH,
                ).start()
            pltpu.make_async_copy(sent_on.at[slot, col], came.at[k, col], n_recv.at[k]).start()

        def all_sent(k, slot):
            part = sent_on.at[slot, pl.ds(0, cols - 1)]
            pltpu.make_async_copy(part, part, n_send.at[k]).wait()

        def combine(k, slot):
            def spread(t, carry):
                at = (t // rows) * g.o
                block = got[k, t].astype(F32)
                for f in range(g.o):
                    for s in range(g.o):
                        start = (f * g.o + s) * g.v
                        tile, phase = start // LANES, start % LANES
                        span = min(tile * LANES + up(phase + g.v), g.wire) - tile * LANES
                        piece = block[:, tile * LANES : tile * LANES + span]
                        if phase:
                            piece = pltpu.roll(piece, span - phase, 1)
                        goal = pl.ds(s * block_rows + at + f, g.a, stride=g.O)
                        mirror[t % rows, goal, :] = piece[:, :LANES]
                return carry

            lax.fori_loop(0, count, spread, 0)
            for n in range(rows):
                mirror_low[:, n * LANES : (n + 1) * LANES] = mirror[n].astype(BF16)
            mine = amp_buf[slot].reshape(g.o * block_rows, g.V)

            def column(n, carry):
                lane = pl.ds(pl.multiple_of(n * 256, 256), 256)
                total[:, lane] = jnp.dot(
                    mirror_low[...], place_ref[:, lane], preferred_element_type=F32
                ) + jnp.dot(mine, fock_ref[:, lane], preferred_element_type=F32)
                return carry

            lax.fori_loop(0, g.wide // 256, column, 0)
            start = first(k)
            lane_of = lax.broadcasted_iota(jnp.int32, (g.pair, LANES), 1)
            for a in range(g.a):
                level = vir_ref[row * g.v + start + a]
                fresh = start + a >= k * g.a
                for i in range(g.o):
                    at = i * block_rows + a * g.O
                    summed = total[at : at + g.O, : g.V] + int_buf[
                        slot, i, a * g.O : (a + 1) * g.O, :
                    ].astype(F32)
                    levels = base_ref[...] + (level - occ_ref[col * g.o + i])
                    value = summed / (levels.astype(F32) * level_step)
                    result[slot, i, a * g.O : (a + 1) * g.O, :] = value.astype(BF16)
                    line[i * g.O : (i + 1) * g.O, : g.V] = jnp.where(fresh, value, 0.0)
                goal = a * g.d
                goal_tile, goal_phase = goal // LANES, goal % LANES
                goal_tiles = up(goal_phase + g.d) // LANES
                for q in range(cols):
                    begin, end = q * g.d, (q + 1) * g.d
                    tiles = max(goal_tiles, -(-end // LANES) - begin // LANES)
                    left = min(begin // LANES, g.wide // LANES - tiles)
                    piece = line[:, left * LANES : (left + tiles) * LANES]
                    shift = (goal_phase - (begin - left * LANES)) % (tiles * LANES)
                    if shift:
                        piece = pltpu.roll(piece, shift, 1)
                    for t in range(goal_tiles):
                        lane = slice((goal_tile + t) * LANES, (goal_tile + t + 1) * LANES)
                        new = piece[:, t * LANES : (t + 1) * LANES]
                        if t == 0 and goal_phase:
                            old = sent_on[slot, q, :, lane].astype(F32)
                            new = jnp.where(lane_of >= goal_phase, new, old)
                        if a == g.a - 1 and t == goal_tiles - 1 and g.nkp > g.nk:
                            new = jnp.where(lane_of < g.nk - (goal_tile + t) * LANES, new, 0.0)
                        sent_on[slot, q, :, lane] = new.astype(BF16)

        def multiply(k, slot):
            pltpu.make_async_copy(came.at[k], came.at[k], n_recv.at[k]).wait()
            slab_load(k, slot).wait()

            def split(m, carry):
                at = pl.ds(pl.multiple_of(m * g.split_rows, 16), g.split_rows)
                parted = pltpu.einshape("tab->atb", slab_buf[slot, at])
                for w in range(g.window):
                    split_buf[w, at, :] = parted[w]
                return carry

            lax.fori_loop(0, g.nk // g.split_rows, split, 0)

            left = came[k].reshape(cols * g.pair, g.nkp)[:, : g.nk]

            def column(w, carry):
                term_ref[w] += jnp.dot(left, split_buf[w], preferred_element_type=F32)
                return carry

            lax.fori_loop(0, g.window, column, 0)

        def reduce():
            for n in range(1, cols):
                peer = (col + n) % cols
                at = pl.ds(pl.multiple_of(peer * g.pair, g.pair), g.pair)
                for w in range(g.window):
                    send_col[n - 1, w] = term_ref[w, at, :].astype(BF16)
                pltpu.make_async_remote_copy(
                    src_ref=send_col.at[n - 1],
                    dst_ref=came_col.at[cols - 1 - n],
                    send_sem=end_sem.at[0],
                    recv_sem=end_sem.at[1],
                    device_id=(row, peer),
                    device_id_type=MESH,
                ).start()
            here = lax.broadcasted_iota(jnp.int32, (g.pair, g.pair), 0)
            there = lax.broadcasted_iota(jnp.int32, (g.pair, g.pair), 1)
            swap = jnp.where(there == (here % g.o) * g.O + here // g.o, 1.0, 0.0).astype(BF16)
            pltpu.make_async_copy(came_col, came_col, end_sem.at[1]).wait()
            at = pl.ds(pl.multiple_of(col * g.pair, g.pair), g.pair)
            for w in range(g.window):
                whole = term_ref[w, at, :]
                for n in range(cols - 1):
                    whole = whole + came_col[n, w].astype(F32)
                whole = jnp.dot(swap, whole.astype(BF16), preferred_element_type=F32)
                for n in range(rows):
                    send_row[n, w] = whole[n * g.each : (n + 1) * g.each].astype(BF16)
            for n in range(1, rows):
                peer = (row + n) % rows
                pltpu.make_async_remote_copy(
                    src_ref=send_row.at[peer],
                    dst_ref=came_row.at[rows - 1 - n],
                    send_sem=end_sem.at[2],
                    recv_sem=end_sem.at[3],
                    device_id=(peer, col),
                    device_id_type=MESH,
                ).start()
            pltpu.make_async_copy(came_row, came_row, end_sem.at[3]).wait()
            for w in range(g.window):
                whole = send_row[row, w].astype(F32)
                for n in range(rows - 1):
                    whole = whole + came_row[n, w].astype(F32)
                ladder_ref[w] = whole
            pltpu.make_async_copy(send_col, send_col, end_sem.at[0]).wait()
            part = send_row.at[pl.ds(0, rows - 1)]
            pltpu.make_async_copy(part, part, end_sem.at[2]).wait()

        for copy in loads(0, 0):
            copy.start()
        for k in range(min(2, g.k)):
            slab_load(k, k).start()
        fock_ref[...] = jnp.zeros_like(fock_ref)
        fock_ref[:, : g.V] = (2.0 * jnp.transpose(raw_ref[...].astype(F32))).astype(BF16)
        down = lax.broadcasted_iota(jnp.int32, (LANES, g.wide), 0)
        gap = lax.broadcasted_iota(jnp.int32, (LANES, g.wide), 1) - down
        for n in range(rows):
            same = jnp.logical_and(gap == n * g.v, down < g.v)
            place_ref[n * LANES : (n + 1) * LANES, :] = jnp.where(same, 1.0, 0.0).astype(BF16)
        base_ref[...] = vir_row_ref[...] - occ_col_ref[...]
        term_ref[...] = jnp.zeros_like(term_ref)
        line[...] = jnp.zeros_like(line)

        def chunk(k, carry):
            slot = k % 2

            @pl.when(k + AHEAD == g.k - 1)
            def _():
                send_blocks(g.k - 1, g.last)

            @pl.when(k + AHEAD < g.k - 1)
            def _():
                send_blocks(k + AHEAD, g.wire)

            @pl.when(k + 1 < g.k)
            def _():
                for copy in loads(k + 1, (k + 1) % 2):
                    copy.start()

            for copy in loads(k, slot):
                copy.wait()

            @pl.when(k < g.k - 1)
            def _():
                arrived(k, g.wire)

            @pl.when(k == g.k - 1)
            def _():
                arrived(g.k - 1, g.last)
                if g.pack:
                    over = g.wire - g.half

                    def unpack(t, carry):
                        block = got[g.k - 1, t, :, : g.half].astype(F32)
                        block = pltpu.roll(block, g.a - g.left, 0)
                        got[g.k - 1, t, :, g.half :] = block[:, :over].astype(BF16)
                        return carry

                    lax.fori_loop(0, count, unpack, 0)


            @pl.when(k >= 2)
            def _():
                all_sent(k - 2, slot)

            combine(k, slot)
            send_amps(k, slot)

            @pl.when(k >= 1)
            def _():
                out_store(k - 1, (k + 1) % 2).wait()

            @pl.when(k < g.k - 1)
            def _():
                out_store(k, slot).start()

            @pl.when(k == g.k - 1)
            def _():
                last_store().start()

            @pl.when(k >= 1)
            def _():
                multiply(k - 1, (k + 1) % 2)

                @pl.when(k + 1 < g.k)
                def _():
                    slab_load(k + 1, (k + 1) % 2).start()

            return carry

        lax.fori_loop(0, g.k, chunk, 0)
        multiply(g.k - 1, (g.k - 1) % 2)
        for k in range(max(0, g.k - 2), g.k):
            all_sent(k, k % 2)
        reduce()
        last_store().wait()

        def drain(k, carry):
            gone(k, g.wire)
            return carry

        lax.fori_loop(0, g.k - 1, drain, 0)
        gone(g.k - 1, g.last)
    slots = 2
    pl.run_scoped(
        turn,
        pltpu.VMEM((g.v * g.O, cols * g.order_width), BF16),
        pltpu.VMEM((g.turn_total, g.V), BF16),
        pltpu.VMEM((max(g.groups) * rows * g.a, g.V), BF16),
        pltpu.VMEM((slots, g.v * g.O, g.V), BF16),
        pltpu.VMEM((slots, g.v * g.O, g.V), BF16),
        pltpu.VMEM((cols, max(g.groups) * rows * g.a, g.wire), BF16),
    )
    pl.run_scoped(
        rest,
        pltpu.VMEM((2, g.cols, g.pair, g.nkp), BF16),
        pltpu.VMEM((2, g.o, block_rows, g.V), BF16),
        pltpu.VMEM((2, g.o, block_rows, g.V), BF16),
        pltpu.VMEM((2, g.nk, g.window, g.V), BF16),
        pltpu.VMEM((g.window, g.nk, g.V), BF16),
        pltpu.VMEM((g.rows, g.o * block_rows, LANES), F32),
        pltpu.VMEM((g.o * block_rows, g.rows * LANES), BF16),
        pltpu.VMEM((g.o * block_rows, g.wide), F32),
        pltpu.VMEM((g.pair, g.wide), F32),
        pltpu.VMEM((2, g.o, block_rows, g.V), BF16),
        pltpu.VMEM((g.window, cols * g.pair, g.V), F32),
        pltpu.VMEM((g.V, g.wide), BF16),
        pltpu.VMEM((rows * LANES, g.wide), BF16),
        pltpu.VMEM((g.O, g.V), jnp.int32),
        pltpu.VMEM((cols - 1, g.window, g.pair, g.V), BF16),
        pltpu.VMEM((rows, g.window, g.each, g.V), BF16),
    )


def main_call(g, amps, ints, slab, fock_virtual, occ_levels, vir_levels):
    count = g.rows * g.cols
    any_space = pl.BlockSpec(memory_space=pl.ANY)
    vmem = pl.BlockSpec(memory_space=pltpu.VMEM)
    smem = pl.BlockSpec(memory_space=pltpu.SMEM)
    dma = pltpu.SemaphoreType.DMA
    out, _, ladder = pl.pallas_call(
        functools.partial(main_kernel, g),
        out_shape=(
            jax.ShapeDtypeStruct((g.o, g.v * g.O, g.V), BF16),
            jax.ShapeDtypeStruct((g.cols, g.turn_total, g.wire), BF16),
            jax.ShapeDtypeStruct((g.window, g.each, g.V), F32),
        ),
        in_specs=[any_space] * 3 + [vmem] * 3 + [smem] * 2,
        out_specs=(any_space, any_space, vmem),
        scratch_shapes=[
            pltpu.VMEM((g.k, count, g.a, g.wire), BF16),
            pltpu.VMEM((g.k, g.cols, g.pair, g.nkp), BF16),
            pltpu.VMEM((g.cols - 1, g.window, g.pair, g.V), BF16),
            pltpu.VMEM((g.rows - 1, g.window, g.each, g.V), BF16),
            dma((g.k,)), dma((g.k,)), dma((g.k,)), dma((g.k,)),
            dma((2, 2)), dma((2,)), dma((2,)), dma((2, 2)), dma(()), dma((4,)),
        ],
        compiler_params=pltpu.CompilerParams(
            collective_id=0, has_side_effects=True, vmem_limit_bytes=67_000_000
        ),
    )(
        amps, ints, slab, fock_virtual, occ_levels.reshape(g.O, 1), vir_levels.reshape(1, g.V),
        occ_levels, vir_levels,
    )
    return out, ladder


def body(rows, cols, amplitudes, integrals, fock_virtual, occ_levels, vir_levels, ladder_ints):
    g = sizes(rows, cols, amplitudes, ladder_ints)
    amps = jnp.transpose(amplitudes, (0, 2, 1, 3)).reshape(g.o, g.v * g.O, g.V)
    ints = jnp.transpose(integrals, (0, 2, 1, 3)).reshape(g.o, g.v * g.O, g.V)
    slab = ladder_ints.reshape(g.v * g.d, g.window, g.V)
    result, ladder = main_call(g, amps, ints, slab, fock_virtual, occ_levels, vir_levels)
    new_amps = jnp.transpose(result.reshape(g.o, g.v, g.O, g.V), (0, 2, 1, 3))
    ladder = ladder.reshape(g.window, g.O // rows, g.o, g.V)
    return (new_amps, jnp.transpose(ladder, (2, 1, 0, 3)).astype(BF16))


def solution(mesh):
    placed = (
        P("col", None, "row", None),
        P("col", None, "row", None),
        P(),
        P(),
        P(),
        P("row", "col", None, None),
    )
    return jax.shard_map(
        functools.partial(body, mesh.shape["row"], mesh.shape["col"]),
        mesh=mesh,
        in_specs=placed,
        out_specs=(P("col", None, "row", None), P("col", "row", None, None)),
        check_vma=False,
    )
```

```python
import functools

import jax
import jax.numpy as jnp
from jax import lax
from jax.experimental import pallas as pl
from jax.experimental.pallas import tpu as pltpu
from jax.sharding import PartitionSpec as P

level_step = 0.1
MESH = pl.DeviceIdType.MESH
LANES = 128
CHUNK = 8
AHEAD = 4
GROUPS = (1, 3, 4, 5)
PLANE = 2
F32 = jnp.float32
BF16 = jnp.bfloat16
NT = (((1,), (1,)), ((), ()))


def up(n, m=LANES):
    return -(-n // m) * m


def partner(k, rows, cols, row, col):
    turn = k // cols
    away = rows // 2 + ((turn + 1) // 2) * (1 - 2 * (turn % 2))
    return ((row + away + rows) % rows, (col + k % cols + 1) % cols)


def greet_all(rows, cols, row, col):
    barrier = pltpu.get_barrier_semaphore()
    count = rows * cols

    def greet(k, carry):
        pl.semaphore_signal(
            barrier, inc=1, device_id=partner(k, rows, cols, row, col), device_id_type=MESH
        )
        return carry

    lax.fori_loop(0, count - 1, greet, 0)
    pl.semaphore_wait(barrier, count - 1)


class Sizes:
    pass


def sizes(rows, cols, amplitudes, ladder_ints):
    g = Sizes()
    g.rows, g.cols = rows, cols
    g.o, g.O, g.v, g.V = amplitudes.shape
    g.window = ladder_ints.shape[2]
    g.d = ladder_ints.shape[1]
    g.a = CHUNK
    g.k = -(-g.v // g.a)
    g.wire = up(g.o * g.o * g.v)
    g.pair = g.o * g.O
    g.nk = g.a * g.d
    g.nkp = up(g.nk)
    g.turn_total = g.k * rows * g.a
    starts = [f * g.o * g.v for f in range(g.o)]
    g.order_width = up(g.o * g.v + max(start % LANES for start in starts))
    g.wire = max([g.wire] + [start // LANES * LANES + g.order_width for start in starts])
    g.groups = []
    while sum(g.groups) < g.k:
        want = GROUPS[min(len(g.groups), len(GROUPS) - 1)]
        g.groups.append(min(want, g.k - sum(g.groups)))
    g.left = g.v - (g.k - 1) * g.a
    g.pack = 2 * g.left == g.a
    g.half = up(g.wire // 2)
    g.last = g.half if g.pack else g.wire
    g.each = g.O // rows * g.o
    g.wide = up(g.V, 256)
    g.split_rows = max(t for t in range(16, 401, 16) if g.nk % t == 0)
    return g


def main_kernel(
    g,
    amps_ref, ints_ref, slab_ref, raw_ref, occ_col_ref, vir_row_ref, occ_ref, vir_ref,
    out_ref, wire_ref, ladder_ref,
    got, came, came_col, came_row,
    x_send, x_recv, n_send, n_recv, in_sem, slab_sem, out_sem, turn_sem, wire_sem, end_sem,
):
    rows, cols = g.rows, g.cols
    count = rows * cols
    row, col = lax.axis_index("row"), lax.axis_index("col")
    block_rows = g.a * g.O

    def first(k):
        return jnp.minimum(k * g.a, g.v - g.a)

    planes = rows // PLANE

    def send_block(k, width, peer_row, peer_col):
        lanes = pl.ds(0, width)
        at = pl.multiple_of((k * rows + peer_row) * g.a, g.a)
        pltpu.make_async_remote_copy(
            src_ref=wire_ref.at[peer_col, pl.ds(at, g.a), lanes],
            dst_ref=got.at[k, col * rows + row, :, lanes],
            send_sem=x_send.at[k],
            recv_sem=x_recv.at[k],
            device_id=(peer_row, peer_col),
            device_id_type=MESH,
        ).start()

    def send_far(k, width):
        def begin(t, carry):
            turn = t // (PLANE * cols)
            away = planes // 2 + ((turn + 1) // 2) * (1 - 2 * (turn % 2))
            plane = (row // PLANE + away + planes) % planes
            core = (t // cols) % PLANE
            send_block(k, width, plane * PLANE + core, (col + t % cols + 1) % cols)
            return carry

        lax.fori_loop(0, (planes - 1) * PLANE * cols, begin, 0)

    def send_near(k, width):
        def begin(t, carry):
            core = (row % PLANE + t // cols + 1) % PLANE
            send_block(k, width, row // PLANE * PLANE + core, (col + t % cols + 1) % cols)
            return carry

        lax.fori_loop(0, PLANE * cols - 1, begin, 0)
        lanes = pl.ds(0, width)
        at = pl.multiple_of((k * rows + row) * g.a, g.a)
        pltpu.make_async_copy(
            wire_ref.at[col, pl.ds(at, g.a), lanes],
            got.at[k, col * rows + row, :, lanes],
            x_recv.at[k],
        ).start()

    def arrived(k, width):
        part = got.at[k, :, :, pl.ds(0, width)]
        pltpu.make_async_copy(part, part, x_recv.at[k]).wait()

    def gone(k, width):
        part = got.at[k, pl.ds(0, count - 1), :, pl.ds(0, width)]
        pltpu.make_async_copy(part, part, x_send.at[k]).wait()

    def turn(order, pick, fock_rows, amp_whole, int_whole, staged):
        def whole(step):
            f, slot = step % g.o, step % 2
            return (
                pltpu.make_async_copy(amps_ref.at[f], amp_whole.at[slot], turn_sem.at[0, slot]),
                pltpu.make_async_copy(ints_ref.at[f], int_whole.at[slot], turn_sem.at[1, slot]),
            )

        steps = len(g.groups) * g.o
        for copy in whole(0):
            copy.start()
        width = cols * g.order_width
        spin = lax.broadcasted_iota(jnp.int32, (g.O, width), 0)
        lane = lax.broadcasted_iota(jnp.int32, (g.O, width), 1)
        offset = lane - (spin // g.o) * g.order_width - (spin % g.o) * g.v

        def order_row(u, carry):
            at = pl.ds(pl.multiple_of(u * g.O, g.O), g.O)
            order[at, :] = jnp.where(offset == u, 1.0, 0.0).astype(BF16)
            return carry

        lax.fori_loop(0, g.v, order_row, 0)
        both = lax.broadcasted_iota(jnp.int32, (2 * g.a, g.V), 0)
        place_of = lax.broadcasted_iota(jnp.int32, (2 * g.a, g.V), 1)
        upper = jnp.where(both >= g.a, 1, 0)
        part = both - upper * g.a
        again = jnp.where(part < g.a - g.left, part + g.left, part) if g.pack else part

        def pick_rows(k, shape):
            def one(n, carry):
                at = pl.ds(pl.multiple_of((k * rows + 2 * n) * g.a, 2 * g.a), 2 * g.a)
                same = place_of - shape - upper * g.v == 2 * n * g.v + first(k)
                pick[at, :] = jnp.where(same, 1.0, 0.0).astype(BF16)
                return carry

            lax.fori_loop(0, rows // 2, one, 0)

        def pick_chunk(k, carry):
            pick_rows(k, part)
            return carry

        lax.fori_loop(0, g.k - 1, pick_chunk, 0)
        pick_rows(g.k - 1, again)
        greet_all(rows, cols, row, col)
        done = 0
        for number, size in enumerate(g.groups):
            height = size * rows * g.a
            at = slice(done * rows * g.a, done * rows * g.a + height)
            staged[:, :height] = jnp.zeros((cols, height, g.wire), BF16)
            fock_rows[:height] = (
                2.0 * jnp.dot(pick[at, :], raw_ref[...], preferred_element_type=F32)
            ).astype(BF16)

            def one(f, carry):
                step = number * g.o + f
                slot = step % 2

                @pl.when(step + 1 < steps)
                def _():
                    for copy in whole(step + 1):
                        copy.start()

                for copy in whole(step):
                    copy.wait()
                turned = lax.dot_general(
                    fock_rows[:height], amp_whole[slot], NT, preferred_element_type=F32
                ) + lax.dot_general(pick[at, :], int_whole[slot], NT, preferred_element_type=F32)
                turned = turned.astype(BF16)
                start = f * (g.o * g.v)
                lanes = pl.ds(pl.multiple_of(start // LANES * LANES, LANES), g.order_width)
                for q in range(cols):
                    piece = jnp.dot(
                        turned,
                        order[:, q * g.order_width : (q + 1) * g.order_width],
                        preferred_element_type=F32,
                    )
                    piece = pltpu.roll(piece, start % LANES, 1)
                    staged[q, :height, lanes] += piece.astype(BF16)
                return carry

            lax.fori_loop(0, g.o, one, 0)
            if g.pack and done + size == g.k:
                over = g.wire - g.half
                tail = slice(height - rows * g.a, height)
                high = lax.broadcasted_iota(jnp.int32, (rows * g.a, over), 0) % g.a < g.a - g.left
                for q in range(cols):
                    staged[q, tail, :over] = jnp.where(
                        high,
                        staged[q, tail, g.half :].astype(F32),
                        staged[q, tail, :over].astype(F32),
                    ).astype(BF16)
            copy = pltpu.make_async_copy(staged.at[:, pl.ds(0, height)], wire_ref.at[:, at], wire_sem)
            copy.start()
            copy.wait()
            for k in range(done, done + size):
                width = g.last if k == g.k - 1 else g.wire
                if k < AHEAD:
                    send_far(k, width)
                send_near(k, width)
            done += size

    def rest(
        sent_on, amp_buf, int_buf, slab_buf, split_buf, mirror, mirror_low, total, line, result,
        term_ref, fock_ref, place_ref, base_ref, send_col, send_row,
    ):
        def loads(k, slot):
            at = pl.ds(pl.multiple_of(first(k) * g.O, g.O), block_rows)
            return (
                pltpu.make_async_copy(amps_ref.at[:, at, :], amp_buf.at[slot], in_sem.at[0, slot]),
                pltpu.make_async_copy(ints_ref.at[:, at, :], int_buf.at[slot], in_sem.at[1, slot]),
            )

        def slab_load(k, slot):
            return pltpu.make_async_copy(
                slab_ref.at[pl.ds(first(k) * g.d, g.nk)], slab_buf.at[slot], slab_sem.at[slot]
            )

        def out_store(k, slot):
            at = pl.ds(pl.multiple_of(first(k) * g.O, g.O), block_rows)
            return pltpu.make_async_copy(result.at[slot], out_ref.at[:, at, :], out_sem.at[slot])

        def last_store():
            height = g.left * g.O
            slot = (g.k - 1) % 2
            return pltpu.make_async_copy(
                result.at[slot, :, pl.ds(block_rows - height, height), :],
                out_ref.at[:, pl.ds((g.k - 1) * g.a * g.O, height), :],
                out_sem.at[slot],
            )

        def send_amps(k, slot, lanes):
            for n in range(1, cols):
                peer = (col + n) % cols
                pltpu.make_async_remote_copy(
                    src_ref=sent_on.at[slot, peer, :, lanes],
                    dst_ref=came.at[k, col, :, lanes],
                    send_sem=n_send.at[k],
                    recv_sem=n_recv.at[k],
                    device_id=(row, peer),
                    device_id_type=MESH,
                ).start()
            pltpu.make_async_copy(
                sent_on.at[slot, col, :, lanes], came.at[k, col, :, lanes], n_recv.at[k]
            ).start()

        def all_sent(k, slot, lanes):
            part = sent_on.at[slot, pl.ds(0, cols - 1), :, lanes]
            pltpu.make_async_copy(part, part, n_send.at[k]).wait()

        def combine(k, slot):
            def spread(t, carry):
                at = (t // rows) * g.o
                block = got[k, t].astype(F32)
                for f in range(g.o):
                    for s in range(g.o):
                        start = (f * g.o + s) * g.v
                        tile, phase = start // LANES, start % LANES
                        span = min(tile * LANES + up(phase + g.v), g.wire) - tile * LANES
                        piece = block[:, tile * LANES : tile * LANES + span]
                        if phase:
                            piece = pltpu.roll(piece, span - phase, 1)
                        goal = pl.ds(s * block_rows + at + f, g.a, stride=g.O)
                        mirror[t % rows, goal, :] = piece[:, :LANES]
                return carry

            lax.fori_loop(0, count, spread, 0)
            for n in range(rows):
                mirror_low[:, n * LANES : (n + 1) * LANES] = mirror[n].astype(BF16)
            mine = amp_buf[slot].reshape(g.o * block_rows, g.V)

            def column(n, carry):
                lane = pl.ds(pl.multiple_of(n * 256, 256), 256)
                total[:, lane] = jnp.dot(
                    mirror_low[...], place_ref[:, lane], preferred_element_type=F32
                ) + jnp.dot(mine, fock_ref[:, lane], preferred_element_type=F32)
                return carry

            lax.fori_loop(0, g.wide // 256, column, 0)
            start = first(k)
            lane_of = lax.broadcasted_iota(jnp.int32, (g.pair, LANES), 1)
            for a in range(g.a):
                level = vir_ref[row * g.v + start + a]
                fresh = start + a >= k * g.a
                for i in range(g.o):
                    at = i * block_rows + a * g.O
                    summed = total[at : at + g.O, : g.V] + int_buf[
                        slot, i, a * g.O : (a + 1) * g.O, :
                    ].astype(F32)
                    levels = base_ref[...] + (level - occ_ref[col * g.o + i])
                    value = summed / (levels.astype(F32) * level_step)
                    result[slot, i, a * g.O : (a + 1) * g.O, :] = value.astype(BF16)
                    line[i * g.O : (i + 1) * g.O, : g.V] = jnp.where(fresh, value, 0.0)
                goal = a * g.d
                goal_tile, goal_phase = goal // LANES, goal % LANES
                goal_tiles = up(goal_phase + g.d) // LANES
                for q in range(cols):
                    begin, end = q * g.d, (q + 1) * g.d
                    tiles = max(goal_tiles, -(-end // LANES) - begin // LANES)
                    left = min(begin // LANES, g.wide // LANES - tiles)
                    piece = line[:, left * LANES : (left + tiles) * LANES]
                    shift = (goal_phase - (begin - left * LANES)) % (tiles * LANES)
                    if shift:
                        piece = pltpu.roll(piece, shift, 1)
                    for t in range(goal_tiles):
                        lane = slice((goal_tile + t) * LANES, (goal_tile + t + 1) * LANES)
                        new = piece[:, t * LANES : (t + 1) * LANES]
                        if t == 0 and goal_phase:
                            old = sent_on[slot, q, :, lane].astype(F32)
                            new = jnp.where(lane_of >= goal_phase, new, old)
                        if a == g.a - 1 and t == goal_tiles - 1 and g.nkp > g.nk:
                            new = jnp.where(lane_of < g.nk - (goal_tile + t) * LANES, new, 0.0)
                        sent_on[slot, q, :, lane] = new.astype(BF16)

        stale = (g.a - g.left) * g.d // LANES * LANES
        every = pl.ds(0, g.nkp)
        valid = pl.ds(stale, g.nkp - stale)
        if stale:
            came[g.k - 1, :, :, :stale] = jnp.zeros((cols, g.pair, stale), BF16)

        def multiply(k, slot, lanes):
            part = came.at[k, :, :, lanes]
            pltpu.make_async_copy(part, part, n_recv.at[k]).wait()
            slab_load(k, slot).wait()

            def split(m, carry):
                at = pl.ds(pl.multiple_of(m * g.split_rows, 16), g.split_rows)
                parted = pltpu.einshape("tab->atb", slab_buf[slot, at])
                for w in range(g.window):
                    split_buf[w, at, :] = parted[w]
                return carry

            lax.fori_loop(0, g.nk // g.split_rows, split, 0)

            left = came[k].reshape(cols * g.pair, g.nkp)[:, : g.nk]

            def column(w, carry):
                term_ref[w] += jnp.dot(left, split_buf[w], preferred_element_type=F32)
                return carry

            lax.fori_loop(0, g.window, column, 0)

        def reduce():
            for n in range(1, cols):
                peer = (col + n) % cols
                at = pl.ds(pl.multiple_of(peer * g.pair, g.pair), g.pair)
                for w in range(g.window):
                    send_col[n - 1, w] = term_ref[w, at, :].astype(BF16)
                pltpu.make_async_remote_copy(
                    src_ref=send_col.at[n - 1],
                    dst_ref=came_col.at[cols - 1 - n],
                    send_sem=end_sem.at[0],
                    recv_sem=end_sem.at[1],
                    device_id=(row, peer),
                    device_id_type=MESH,
                ).start()
            here = lax.broadcasted_iota(jnp.int32, (g.pair, g.pair), 0)
            there = lax.broadcasted_iota(jnp.int32, (g.pair, g.pair), 1)
            swap = jnp.where(there == (here % g.o) * g.O + here // g.o, 1.0, 0.0).astype(BF16)
            pltpu.make_async_copy(came_col, came_col, end_sem.at[1]).wait()
            at = pl.ds(pl.multiple_of(col * g.pair, g.pair), g.pair)
            for w in range(g.window):
                whole = term_ref[w, at, :]
                for n in range(cols - 1):
                    whole = whole + came_col[n, w].astype(F32)
                whole = jnp.dot(swap, whole.astype(BF16), preferred_element_type=F32)
                for n in range(rows):
                    send_row[n, w] = whole[n * g.each : (n + 1) * g.each].astype(BF16)
            for n in range(1, rows):
                peer = (row + n) % rows
                pltpu.make_async_remote_copy(
                    src_ref=send_row.at[peer],
                    dst_ref=came_row.at[rows - 1 - n],
                    send_sem=end_sem.at[2],
                    recv_sem=end_sem.at[3],
                    device_id=(peer, col),
                    device_id_type=MESH,
                ).start()
            pltpu.make_async_copy(came_row, came_row, end_sem.at[3]).wait()
            for w in range(g.window):
                whole = send_row[row, w].astype(F32)
                for n in range(rows - 1):
                    whole = whole + came_row[n, w].astype(F32)
                ladder_ref[w] = whole
            pltpu.make_async_copy(send_col, send_col, end_sem.at[0]).wait()
            part = send_row.at[pl.ds(0, rows - 1)]
            pltpu.make_async_copy(part, part, end_sem.at[2]).wait()

        for copy in loads(0, 0):
            copy.start()
        for k in range(min(2, g.k)):
            slab_load(k, k).start()
        fock_ref[...] = jnp.zeros_like(fock_ref)
        fock_ref[:, : g.V] = (2.0 * jnp.transpose(raw_ref[...].astype(F32))).astype(BF16)
        down = lax.broadcasted_iota(jnp.int32, (LANES, g.wide), 0)
        gap = lax.broadcasted_iota(jnp.int32, (LANES, g.wide), 1) - down
        for n in range(rows):
            same = jnp.logical_and(gap == n * g.v, down < g.v)
            place_ref[n * LANES : (n + 1) * LANES, :] = jnp.where(same, 1.0, 0.0).astype(BF16)
        base_ref[...] = vir_row_ref[...] - occ_col_ref[...]
        term_ref[...] = jnp.zeros_like(term_ref)
        line[...] = jnp.zeros_like(line)

        def chunk(k, carry):
            slot = k % 2

            @pl.when(k + AHEAD == g.k - 1)
            def _():
                send_far(g.k - 1, g.last)

            @pl.when(k + AHEAD < g.k - 1)
            def _():
                send_far(k + AHEAD, g.wire)

            @pl.when(k + 1 < g.k)
            def _():
                for copy in loads(k + 1, (k + 1) % 2):
                    copy.start()

            for copy in loads(k, slot):
                copy.wait()

            @pl.when(k < g.k - 1)
            def _():
                arrived(k, g.wire)

            @pl.when(k == g.k - 1)
            def _():
                arrived(g.k - 1, g.last)
                if g.pack:
                    over = g.wire - g.half

                    def unpack(t, carry):
                        block = got[g.k - 1, t, :, : g.half].astype(F32)
                        block = pltpu.roll(block, g.a - g.left, 0)
                        got[g.k - 1, t, :, g.half :] = block[:, :over].astype(BF16)
                        return carry

                    lax.fori_loop(0, count, unpack, 0)


            @pl.when(k >= 2)
            def _():
                all_sent(k - 2, slot, every)

            combine(k, slot)
            @pl.when(k < g.k - 1)
            def _():
                send_amps(k, slot, every)

            @pl.when(k == g.k - 1)
            def _():
                send_amps(g.k - 1, slot, valid)

            @pl.when(k >= 1)
            def _():
                out_store(k - 1, (k + 1) % 2).wait()

            @pl.when(k < g.k - 1)
            def _():
                out_store(k, slot).start()

            @pl.when(k == g.k - 1)
            def _():
                last_store().start()

            @pl.when(k >= 1)
            def _():
                multiply(k - 1, (k + 1) % 2, every)

                @pl.when(k + 1 < g.k)
                def _():
                    slab_load(k + 1, (k + 1) % 2).start()

            return carry

        lax.fori_loop(0, g.k, chunk, 0)
        multiply(g.k - 1, (g.k - 1) % 2, valid)
        for k in range(max(0, g.k - 2), g.k):
            all_sent(k, k % 2, valid if k == g.k - 1 else every)
        reduce()
        last_store().wait()

        def drain(k, carry):
            gone(k, g.wire)
            return carry

        lax.fori_loop(0, g.k - 1, drain, 0)
        gone(g.k - 1, g.last)
    slots = 2
    pl.run_scoped(
        turn,
        pltpu.VMEM((g.v * g.O, cols * g.order_width), BF16),
        pltpu.VMEM((g.turn_total, g.V), BF16),
        pltpu.VMEM((max(g.groups) * rows * g.a, g.V), BF16),
        pltpu.VMEM((slots, g.v * g.O, g.V), BF16),
        pltpu.VMEM((slots, g.v * g.O, g.V), BF16),
        pltpu.VMEM((cols, max(g.groups) * rows * g.a, g.wire), BF16),
    )
    pl.run_scoped(
        rest,
        pltpu.VMEM((2, g.cols, g.pair, g.nkp), BF16),
        pltpu.VMEM((2, g.o, block_rows, g.V), BF16),
        pltpu.VMEM((2, g.o, block_rows, g.V), BF16),
        pltpu.VMEM((2, g.nk, g.window, g.V), BF16),
        pltpu.VMEM((g.window, g.nk, g.V), BF16),
        pltpu.VMEM((g.rows, g.o * block_rows, LANES), F32),
        pltpu.VMEM((g.o * block_rows, g.rows * LANES), BF16),
        pltpu.VMEM((g.o * block_rows, g.wide), F32),
        pltpu.VMEM((g.pair, g.wide), F32),
        pltpu.VMEM((2, g.o, block_rows, g.V), BF16),
        pltpu.VMEM((g.window, cols * g.pair, g.V), F32),
        pltpu.VMEM((g.V, g.wide), BF16),
        pltpu.VMEM((rows * LANES, g.wide), BF16),
        pltpu.VMEM((g.O, g.V), jnp.int32),
        pltpu.VMEM((cols - 1, g.window, g.pair, g.V), BF16),
        pltpu.VMEM((rows, g.window, g.each, g.V), BF16),
    )


def main_call(g, amps, ints, slab, fock_virtual, occ_levels, vir_levels):
    count = g.rows * g.cols
    any_space = pl.BlockSpec(memory_space=pl.ANY)
    vmem = pl.BlockSpec(memory_space=pltpu.VMEM)
    smem = pl.BlockSpec(memory_space=pltpu.SMEM)
    dma = pltpu.SemaphoreType.DMA
    out, _, ladder = pl.pallas_call(
        functools.partial(main_kernel, g),
        out_shape=(
            jax.ShapeDtypeStruct((g.o, g.v * g.O, g.V), BF16),
            jax.ShapeDtypeStruct((g.cols, g.turn_total, g.wire), BF16),
            jax.ShapeDtypeStruct((g.window, g.each, g.V), F32),
        ),
        in_specs=[any_space] * 3 + [vmem] * 3 + [smem] * 2,
        out_specs=(any_space, any_space, vmem),
        scratch_shapes=[
            pltpu.VMEM((g.k, count, g.a, g.wire), BF16),
            pltpu.VMEM((g.k, g.cols, g.pair, g.nkp), BF16),
            pltpu.VMEM((g.cols - 1, g.window, g.pair, g.V), BF16),
            pltpu.VMEM((g.rows - 1, g.window, g.each, g.V), BF16),
            dma((g.k,)), dma((g.k,)), dma((g.k,)), dma((g.k,)),
            dma((2, 2)), dma((2,)), dma((2,)), dma((2, 2)), dma(()), dma((4,)),
        ],
        compiler_params=pltpu.CompilerParams(
            collective_id=0, has_side_effects=True, vmem_limit_bytes=67_000_000
        ),
    )(
        amps, ints, slab, fock_virtual, occ_levels.reshape(g.O, 1), vir_levels.reshape(1, g.V),
        occ_levels, vir_levels,
    )
    return out, ladder


def body(rows, cols, amplitudes, integrals, fock_virtual, occ_levels, vir_levels, ladder_ints):
    g = sizes(rows, cols, amplitudes, ladder_ints)
    amps = jnp.transpose(amplitudes, (0, 2, 1, 3)).reshape(g.o, g.v * g.O, g.V)
    ints = jnp.transpose(integrals, (0, 2, 1, 3)).reshape(g.o, g.v * g.O, g.V)
    slab = ladder_ints.reshape(g.v * g.d, g.window, g.V)
    result, ladder = main_call(g, amps, ints, slab, fock_virtual, occ_levels, vir_levels)
    new_amps = jnp.transpose(result.reshape(g.o, g.v, g.O, g.V), (0, 2, 1, 3))
    ladder = ladder.reshape(g.window, g.O // rows, g.o, g.V)
    return (new_amps, jnp.transpose(ladder, (2, 1, 0, 3)).astype(BF16))


def solution(mesh):
    placed = (
        P("col", None, "row", None),
        P("col", None, "row", None),
        P(),
        P(),
        P(),
        P("row", "col", None, None),
    )
    return jax.shard_map(
        functools.partial(body, mesh.shape["row"], mesh.shape["col"]),
        mesh=mesh,
        in_specs=placed,
        out_specs=(P("col", None, "row", None), P("col", "row", None, None)),
        check_vma=False,
    )
```

```python
import functools

import jax
import jax.numpy as jnp
from jax import lax
from jax.experimental import pallas as pl
from jax.experimental.pallas import tpu as pltpu
from jax.sharding import PartitionSpec as P

level_step = 0.1
MESH = pl.DeviceIdType.MESH
LANES = 128
CHUNK = 8
AHEAD = 4
HOLD = 3
GROUPS = (1, 3, 4, 5)
PLANE = 2
F32 = jnp.float32
BF16 = jnp.bfloat16
NT = (((1,), (1,)), ((), ()))


def up(n, m=LANES):
    return -(-n // m) * m


def partner(k, rows, cols, row, col):
    turn = k // cols
    away = rows // 2 + ((turn + 1) // 2) * (1 - 2 * (turn % 2))
    return ((row + away + rows) % rows, (col + k % cols + 1) % cols)


def greet_all(rows, cols, row, col):
    barrier = pltpu.get_barrier_semaphore()
    count = rows * cols

    def greet(k, carry):
        pl.semaphore_signal(
            barrier, inc=1, device_id=partner(k, rows, cols, row, col), device_id_type=MESH
        )
        return carry

    lax.fori_loop(0, count - 1, greet, 0)
    pl.semaphore_wait(barrier, count - 1)


class Sizes:
    pass


def sizes(rows, cols, amplitudes, ladder_ints):
    g = Sizes()
    g.rows, g.cols = rows, cols
    g.o, g.O, g.v, g.V = amplitudes.shape
    g.window = ladder_ints.shape[2]
    g.d = ladder_ints.shape[1]
    g.a = CHUNK
    g.k = -(-g.v // g.a)
    g.wire = up(g.o * g.o * g.v)
    g.pair = g.o * g.O
    g.nk = g.a * g.d
    g.nkp = up(g.nk)
    g.turn_total = g.k * rows * g.a
    starts = [f * g.o * g.v for f in range(g.o)]
    g.order_width = up(g.o * g.v + max(start % LANES for start in starts))
    g.wire = max([g.wire] + [start // LANES * LANES + g.order_width for start in starts])
    g.groups = []
    while sum(g.groups) < g.k:
        want = GROUPS[min(len(g.groups), len(GROUPS) - 1)]
        g.groups.append(min(want, g.k - sum(g.groups)))
    g.left = g.v - (g.k - 1) * g.a
    g.pack = 2 * g.left == g.a
    g.half = up(g.wire // 2)
    g.last = g.half if g.pack else g.wire
    g.each = g.O // rows * g.o
    g.wide = up(g.V, 256)
    g.split_rows = max(t for t in range(16, 401, 16) if g.nk % t == 0)
    return g


def main_kernel(
    g,
    amps_ref, ints_ref, slab_ref, raw_ref, occ_col_ref, vir_row_ref, occ_ref, vir_ref,
    out_ref, wire_ref, ladder_ref,
    got, came, came_col, came_row,
    x_send, x_recv, n_send, n_recv, in_sem, slab_sem, out_sem, turn_sem, wire_sem, end_sem,
):
    rows, cols = g.rows, g.cols
    count = rows * cols
    row, col = lax.axis_index("row"), lax.axis_index("col")
    block_rows = g.a * g.O

    def first(k):
        return jnp.minimum(k * g.a, g.v - g.a)

    planes = rows // PLANE

    def send_block(k, width, peer_row, peer_col):
        lanes = pl.ds(0, width)
        at = pl.multiple_of((k * rows + peer_row) * g.a, g.a)
        pltpu.make_async_remote_copy(
            src_ref=wire_ref.at[peer_col, pl.ds(at, g.a), lanes],
            dst_ref=got.at[k, col * rows + row, :, lanes],
            send_sem=x_send.at[k],
            recv_sem=x_recv.at[k],
            device_id=(peer_row, peer_col),
            device_id_type=MESH,
        ).start()

    def send_far(k, width):
        def begin(t, carry):
            turn = t // (PLANE * cols)
            away = planes // 2 + ((turn + 1) // 2) * (1 - 2 * (turn % 2))
            plane = (row // PLANE + away + planes) % planes
            core = (t // cols) % PLANE
            send_block(k, width, plane * PLANE + core, (col + t % cols + 1) % cols)
            return carry

        lax.fori_loop(0, (planes - 1) * PLANE * cols, begin, 0)

    def send_near(k, width):
        def begin(t, carry):
            core = (row % PLANE + t // cols + 1) % PLANE
            send_block(k, width, row // PLANE * PLANE + core, (col + t % cols + 1) % cols)
            return carry

        lax.fori_loop(0, PLANE * cols - 1, begin, 0)
        lanes = pl.ds(0, width)
        at = pl.multiple_of((k * rows + row) * g.a, g.a)
        pltpu.make_async_copy(
            wire_ref.at[col, pl.ds(at, g.a), lanes],
            got.at[k, col * rows + row, :, lanes],
            x_recv.at[k],
        ).start()

    def arrived(k, width):
        part = got.at[k, :, :, pl.ds(0, width)]
        pltpu.make_async_copy(part, part, x_recv.at[k]).wait()

    def gone(k, width):
        part = got.at[k, pl.ds(0, count - 1), :, pl.ds(0, width)]
        pltpu.make_async_copy(part, part, x_send.at[k]).wait()

    def turn(order, pick, fock_rows, amp_whole, int_whole, staged):
        def whole(step):
            f, slot = step % g.o, step % 2
            return (
                pltpu.make_async_copy(amps_ref.at[f], amp_whole.at[slot], turn_sem.at[0, slot]),
                pltpu.make_async_copy(ints_ref.at[f], int_whole.at[slot], turn_sem.at[1, slot]),
            )

        steps = len(g.groups) * g.o
        for copy in whole(0):
            copy.start()
        width = cols * g.order_width
        spin = lax.broadcasted_iota(jnp.int32, (g.O, width), 0)
        lane = lax.broadcasted_iota(jnp.int32, (g.O, width), 1)
        offset = lane - (spin // g.o) * g.order_width - (spin % g.o) * g.v

        def order_row(u, carry):
            at = pl.ds(pl.multiple_of(u * g.O, g.O), g.O)
            order[at, :] = jnp.where(offset == u, 1.0, 0.0).astype(BF16)
            return carry

        lax.fori_loop(0, g.v, order_row, 0)
        both = lax.broadcasted_iota(jnp.int32, (2 * g.a, g.V), 0)
        place_of = lax.broadcasted_iota(jnp.int32, (2 * g.a, g.V), 1)
        upper = jnp.where(both >= g.a, 1, 0)
        part = both - upper * g.a
        again = jnp.where(part < g.a - g.left, part + g.left, part) if g.pack else part

        def pick_rows(k, shape):
            def one(n, carry):
                at = pl.ds(pl.multiple_of((k * rows + 2 * n) * g.a, 2 * g.a), 2 * g.a)
                same = place_of - shape - upper * g.v == 2 * n * g.v + first(k)
                pick[at, :] = jnp.where(same, 1.0, 0.0).astype(BF16)
                return carry

            lax.fori_loop(0, rows // 2, one, 0)

        def pick_chunk(k, carry):
            pick_rows(k, part)
            return carry

        lax.fori_loop(0, g.k - 1, pick_chunk, 0)
        pick_rows(g.k - 1, again)
        greet_all(rows, cols, row, col)
        done = 0
        for number, size in enumerate(g.groups):
            height = size * rows * g.a
            at = slice(done * rows * g.a, done * rows * g.a + height)
            staged[:, :height] = jnp.zeros((cols, height, g.wire), BF16)
            fock_rows[:height] = (
                2.0 * jnp.dot(pick[at, :], raw_ref[...], preferred_element_type=F32)
            ).astype(BF16)

            def one(f, carry):
                step = number * g.o + f
                slot = step % 2

                @pl.when(step + 1 < steps)
                def _():
                    for copy in whole(step + 1):
                        copy.start()

                for copy in whole(step):
                    copy.wait()
                turned = lax.dot_general(
                    fock_rows[:height], amp_whole[slot], NT, preferred_element_type=F32
                ) + lax.dot_general(pick[at, :], int_whole[slot], NT, preferred_element_type=F32)
                turned = turned.astype(BF16)
                start = f * (g.o * g.v)
                lanes = pl.ds(pl.multiple_of(start // LANES * LANES, LANES), g.order_width)
                for q in range(cols):
                    piece = jnp.dot(
                        turned,
                        order[:, q * g.order_width : (q + 1) * g.order_width],
                        preferred_element_type=F32,
                    )
                    piece = pltpu.roll(piece, start % LANES, 1)
                    staged[q, :height, lanes] += piece.astype(BF16)
                return carry

            lax.fori_loop(0, g.o, one, 0)
            if g.pack and done + size == g.k:
                over = g.wire - g.half
                tail = slice(height - rows * g.a, height)
                high = lax.broadcasted_iota(jnp.int32, (rows * g.a, over), 0) % g.a < g.a - g.left
                for q in range(cols):
                    staged[q, tail, :over] = jnp.where(
                        high,
                        staged[q, tail, g.half :].astype(F32),
                        staged[q, tail, :over].astype(F32),
                    ).astype(BF16)
            copy = pltpu.make_async_copy(staged.at[:, pl.ds(0, height)], wire_ref.at[:, at], wire_sem)
            copy.start()
            copy.wait()
            for k in range(done, done + size):
                width = g.last if k == g.k - 1 else g.wire
                if k < AHEAD:
                    send_far(k, width)
                send_near(k, width)
            done += size

    def rest(
        sent_on, amp_buf, int_buf, slab_buf, split_buf, mirror, mirror_low, total, line, result,
        term_ref, fock_ref, place_ref, base_ref, send_col, send_row,
    ):
        def loads(k, slot):
            at = pl.ds(pl.multiple_of(first(k) * g.O, g.O), block_rows)
            return (
                pltpu.make_async_copy(amps_ref.at[:, at, :], amp_buf.at[slot], in_sem.at[0, slot]),
                pltpu.make_async_copy(ints_ref.at[:, at, :], int_buf.at[slot], in_sem.at[1, slot]),
            )

        def slab_load(k, slot):
            return pltpu.make_async_copy(
                slab_ref.at[pl.ds(first(k) * g.d, g.nk)], slab_buf.at[slot], slab_sem.at[slot]
            )

        def out_store(k, slot):
            at = pl.ds(pl.multiple_of(first(k) * g.O, g.O), block_rows)
            return pltpu.make_async_copy(result.at[slot], out_ref.at[:, at, :], out_sem.at[slot])

        def last_store():
            height = g.left * g.O
            slot = (g.k - 1) % 2
            return pltpu.make_async_copy(
                result.at[slot, :, pl.ds(block_rows - height, height), :],
                out_ref.at[:, pl.ds((g.k - 1) * g.a * g.O, height), :],
                out_sem.at[slot],
            )

        def send_amps(k, slot, lanes):
            for n in range(1, cols):
                peer = (col + n) % cols
                pltpu.make_async_remote_copy(
                    src_ref=sent_on.at[slot, peer, :, lanes],
                    dst_ref=came.at[k, col, :, lanes],
                    send_sem=n_send.at[k],
                    recv_sem=n_recv.at[k],
                    device_id=(row, peer),
                    device_id_type=MESH,
                ).start()
            pltpu.make_async_copy(
                sent_on.at[slot, col, :, lanes], came.at[k, col, :, lanes], n_recv.at[k]
            ).start()

        def all_sent(k, slot, lanes):
            part = sent_on.at[slot, pl.ds(0, cols - 1), :, lanes]
            pltpu.make_async_copy(part, part, n_send.at[k]).wait()

        def combine(k, slot):
            hold = k % HOLD
            def spread(t, carry):
                at = (t // rows) * g.o
                block = got[k, t].astype(F32)
                for f in range(g.o):
                    for s in range(g.o):
                        start = (f * g.o + s) * g.v
                        tile, phase = start // LANES, start % LANES
                        span = min(tile * LANES + up(phase + g.v), g.wire) - tile * LANES
                        piece = block[:, tile * LANES : tile * LANES + span]
                        if phase:
                            piece = pltpu.roll(piece, span - phase, 1)
                        goal = pl.ds(s * block_rows + at + f, g.a, stride=g.O)
                        mirror[t % rows, goal, :] = piece[:, :LANES]
                return carry

            lax.fori_loop(0, count, spread, 0)
            for n in range(rows):
                mirror_low[:, n * LANES : (n + 1) * LANES] = mirror[n].astype(BF16)
            mine = amp_buf[slot].reshape(g.o * block_rows, g.V)

            def column(n, carry):
                lane = pl.ds(pl.multiple_of(n * 256, 256), 256)
                total[:, lane] = jnp.dot(
                    mirror_low[...], place_ref[:, lane], preferred_element_type=F32
                ) + jnp.dot(mine, fock_ref[:, lane], preferred_element_type=F32)
                return carry

            lax.fori_loop(0, g.wide // 256, column, 0)
            start = first(k)
            lane_of = lax.broadcasted_iota(jnp.int32, (g.pair, LANES), 1)
            for a in range(g.a):
                level = vir_ref[row * g.v + start + a]
                fresh = start + a >= k * g.a
                for i in range(g.o):
                    at = i * block_rows + a * g.O
                    summed = total[at : at + g.O, : g.V] + int_buf[
                        slot, i, a * g.O : (a + 1) * g.O, :
                    ].astype(F32)
                    levels = base_ref[...] + (level - occ_ref[col * g.o + i])
                    value = summed / (levels.astype(F32) * level_step)
                    result[slot, i, a * g.O : (a + 1) * g.O, :] = value.astype(BF16)
                    line[i * g.O : (i + 1) * g.O, : g.V] = jnp.where(fresh, value, 0.0)
                goal = a * g.d
                goal_tile, goal_phase = goal // LANES, goal % LANES
                goal_tiles = up(goal_phase + g.d) // LANES
                for q in range(cols):
                    begin, end = q * g.d, (q + 1) * g.d
                    tiles = max(goal_tiles, -(-end // LANES) - begin // LANES)
                    left = min(begin // LANES, g.wide // LANES - tiles)
                    piece = line[:, left * LANES : (left + tiles) * LANES]
                    shift = (goal_phase - (begin - left * LANES)) % (tiles * LANES)
                    if shift:
                        piece = pltpu.roll(piece, shift, 1)
                    for t in range(goal_tiles):
                        lane = slice((goal_tile + t) * LANES, (goal_tile + t + 1) * LANES)
                        new = piece[:, t * LANES : (t + 1) * LANES]
                        if t == 0 and goal_phase:
                            old = sent_on[hold, q, :, lane].astype(F32)
                            new = jnp.where(lane_of >= goal_phase, new, old)
                        if a == g.a - 1 and t == goal_tiles - 1 and g.nkp > g.nk:
                            new = jnp.where(lane_of < g.nk - (goal_tile + t) * LANES, new, 0.0)
                        sent_on[hold, q, :, lane] = new.astype(BF16)

        stale = (g.a - g.left) * g.d // LANES * LANES
        every = pl.ds(0, g.nkp)
        valid = pl.ds(stale, g.nkp - stale)
        if stale:
            came[g.k - 1, :, :, :stale] = jnp.zeros((cols, g.pair, stale), BF16)

        def multiply(k, slot, lanes):
            part = came.at[k, :, :, lanes]
            pltpu.make_async_copy(part, part, n_recv.at[k]).wait()
            slab_load(k, slot).wait()

            def split(m, carry):
                at = pl.ds(pl.multiple_of(m * g.split_rows, 16), g.split_rows)
                parted = pltpu.einshape("tab->atb", slab_buf[slot, at])
                for w in range(g.window):
                    split_buf[w, at, :] = parted[w]
                return carry

            lax.fori_loop(0, g.nk // g.split_rows, split, 0)

            left = came[k].reshape(cols * g.pair, g.nkp)[:, : g.nk]

            def column(w, carry):
                term_ref[w] += jnp.dot(left, split_buf[w], preferred_element_type=F32)
                return carry

            lax.fori_loop(0, g.window, column, 0)

        def reduce():
            for n in range(1, cols):
                peer = (col + n) % cols
                at = pl.ds(pl.multiple_of(peer * g.pair, g.pair), g.pair)
                for w in range(g.window):
                    send_col[n - 1, w] = term_ref[w, at, :].astype(BF16)
                pltpu.make_async_remote_copy(
                    src_ref=send_col.at[n - 1],
                    dst_ref=came_col.at[cols - 1 - n],
                    send_sem=end_sem.at[0],
                    recv_sem=end_sem.at[1],
                    device_id=(row, peer),
                    device_id_type=MESH,
                ).start()
            here = lax.broadcasted_iota(jnp.int32, (g.pair, g.pair), 0)
            there = lax.broadcasted_iota(jnp.int32, (g.pair, g.pair), 1)
            swap = jnp.where(there == (here % g.o) * g.O + here // g.o, 1.0, 0.0).astype(BF16)
            pltpu.make_async_copy(came_col, came_col, end_sem.at[1]).wait()
            at = pl.ds(pl.multiple_of(col * g.pair, g.pair), g.pair)
            for w in range(g.window):
                whole = term_ref[w, at, :]
                for n in range(cols - 1):
                    whole = whole + came_col[n, w].astype(F32)
                whole = jnp.dot(swap, whole.astype(BF16), preferred_element_type=F32)
                for n in range(rows):
                    send_row[n, w] = whole[n * g.each : (n + 1) * g.each].astype(BF16)
            for n in range(1, rows):
                peer = (row + n) % rows
                pltpu.make_async_remote_copy(
                    src_ref=send_row.at[peer],
                    dst_ref=came_row.at[rows - 1 - n],
                    send_sem=end_sem.at[2],
                    recv_sem=end_sem.at[3],
                    device_id=(peer, col),
                    device_id_type=MESH,
                ).start()
            pltpu.make_async_copy(came_row, came_row, end_sem.at[3]).wait()
            for w in range(g.window):
                whole = send_row[row, w].astype(F32)
                for n in range(rows - 1):
                    whole = whole + came_row[n, w].astype(F32)
                ladder_ref[w] = whole
            pltpu.make_async_copy(send_col, send_col, end_sem.at[0]).wait()
            part = send_row.at[pl.ds(0, rows - 1)]
            pltpu.make_async_copy(part, part, end_sem.at[2]).wait()

        for copy in loads(0, 0):
            copy.start()
        for k in range(min(2, g.k)):
            slab_load(k, k).start()
        fock_ref[...] = jnp.zeros_like(fock_ref)
        fock_ref[:, : g.V] = (2.0 * jnp.transpose(raw_ref[...].astype(F32))).astype(BF16)
        down = lax.broadcasted_iota(jnp.int32, (LANES, g.wide), 0)
        gap = lax.broadcasted_iota(jnp.int32, (LANES, g.wide), 1) - down
        for n in range(rows):
            same = jnp.logical_and(gap == n * g.v, down < g.v)
            place_ref[n * LANES : (n + 1) * LANES, :] = jnp.where(same, 1.0, 0.0).astype(BF16)
        base_ref[...] = vir_row_ref[...] - occ_col_ref[...]
        term_ref[...] = jnp.zeros_like(term_ref)
        line[...] = jnp.zeros_like(line)

        def chunk(k, carry):
            slot = k % 2

            @pl.when(k + AHEAD == g.k - 1)
            def _():
                send_far(g.k - 1, g.last)

            @pl.when(k + AHEAD < g.k - 1)
            def _():
                send_far(k + AHEAD, g.wire)

            @pl.when(k + 1 < g.k)
            def _():
                for copy in loads(k + 1, (k + 1) % 2):
                    copy.start()

            for copy in loads(k, slot):
                copy.wait()

            @pl.when(k < g.k - 1)
            def _():
                arrived(k, g.wire)

            @pl.when(k == g.k - 1)
            def _():
                arrived(g.k - 1, g.last)
                if g.pack:
                    over = g.wire - g.half

                    def unpack(t, carry):
                        block = got[g.k - 1, t, :, : g.half].astype(F32)
                        block = pltpu.roll(block, g.a - g.left, 0)
                        got[g.k - 1, t, :, g.half :] = block[:, :over].astype(BF16)
                        return carry

                    lax.fori_loop(0, count, unpack, 0)


            @pl.when(k >= HOLD)
            def _():
                all_sent(k - HOLD, k % HOLD, every)

            combine(k, slot)
            @pl.when(k < g.k - 1)
            def _():
                send_amps(k, k % HOLD, every)

            @pl.when(k == g.k - 1)
            def _():
                send_amps(g.k - 1, (g.k - 1) % HOLD, valid)

            @pl.when(k >= 1)
            def _():
                out_store(k - 1, (k + 1) % 2).wait()

            @pl.when(k < g.k - 1)
            def _():
                out_store(k, slot).start()

            @pl.when(k == g.k - 1)
            def _():
                last_store().start()

            @pl.when(k >= 2)
            def _():
                multiply(k - 2, slot, every)
                slab_load(k, slot).start()

            return carry

        lax.fori_loop(0, g.k, chunk, 0)
        for k in range(max(0, g.k - 2), g.k):
            multiply(k, k % 2, valid if k == g.k - 1 else every)
        for k in range(max(0, g.k - HOLD), g.k):
            all_sent(k, k % HOLD, valid if k == g.k - 1 else every)
        reduce()
        last_store().wait()

        def drain(k, carry):
            gone(k, g.wire)
            return carry

        lax.fori_loop(0, g.k - 1, drain, 0)
        gone(g.k - 1, g.last)
    slots = 2
    pl.run_scoped(
        turn,
        pltpu.VMEM((g.v * g.O, cols * g.order_width), BF16),
        pltpu.VMEM((g.turn_total, g.V), BF16),
        pltpu.VMEM((max(g.groups) * rows * g.a, g.V), BF16),
        pltpu.VMEM((slots, g.v * g.O, g.V), BF16),
        pltpu.VMEM((slots, g.v * g.O, g.V), BF16),
        pltpu.VMEM((cols, max(g.groups) * rows * g.a, g.wire), BF16),
    )
    pl.run_scoped(
        rest,
        pltpu.VMEM((HOLD, g.cols, g.pair, g.nkp), BF16),
        pltpu.VMEM((2, g.o, block_rows, g.V), BF16),
        pltpu.VMEM((2, g.o, block_rows, g.V), BF16),
        pltpu.VMEM((2, g.nk, g.window, g.V), BF16),
        pltpu.VMEM((g.window, g.nk, g.V), BF16),
        pltpu.VMEM((g.rows, g.o * block_rows, LANES), F32),
        pltpu.VMEM((g.o * block_rows, g.rows * LANES), BF16),
        pltpu.VMEM((g.o * block_rows, g.wide), F32),
        pltpu.VMEM((g.pair, g.wide), F32),
        pltpu.VMEM((2, g.o, block_rows, g.V), BF16),
        pltpu.VMEM((g.window, cols * g.pair, g.V), F32),
        pltpu.VMEM((g.V, g.wide), BF16),
        pltpu.VMEM((rows * LANES, g.wide), BF16),
        pltpu.VMEM((g.O, g.V), jnp.int32),
        pltpu.VMEM((cols - 1, g.window, g.pair, g.V), BF16),
        pltpu.VMEM((rows, g.window, g.each, g.V), BF16),
    )


def main_call(g, amps, ints, slab, fock_virtual, occ_levels, vir_levels):
    count = g.rows * g.cols
    any_space = pl.BlockSpec(memory_space=pl.ANY)
    vmem = pl.BlockSpec(memory_space=pltpu.VMEM)
    smem = pl.BlockSpec(memory_space=pltpu.SMEM)
    dma = pltpu.SemaphoreType.DMA
    out, _, ladder = pl.pallas_call(
        functools.partial(main_kernel, g),
        out_shape=(
            jax.ShapeDtypeStruct((g.o, g.v * g.O, g.V), BF16),
            jax.ShapeDtypeStruct((g.cols, g.turn_total, g.wire), BF16),
            jax.ShapeDtypeStruct((g.window, g.each, g.V), F32),
        ),
        in_specs=[any_space] * 3 + [vmem] * 3 + [smem] * 2,
        out_specs=(any_space, any_space, vmem),
        scratch_shapes=[
            pltpu.VMEM((g.k, count, g.a, g.wire), BF16),
            pltpu.VMEM((g.k, g.cols, g.pair, g.nkp), BF16),
            pltpu.VMEM((g.cols - 1, g.window, g.pair, g.V), BF16),
            pltpu.VMEM((g.rows - 1, g.window, g.each, g.V), BF16),
            dma((g.k,)), dma((g.k,)), dma((g.k,)), dma((g.k,)),
            dma((2, 2)), dma((2,)), dma((2,)), dma((2, 2)), dma(()), dma((4,)),
        ],
        compiler_params=pltpu.CompilerParams(
            collective_id=0, has_side_effects=True, vmem_limit_bytes=67_000_000
        ),
    )(
        amps, ints, slab, fock_virtual, occ_levels.reshape(g.O, 1), vir_levels.reshape(1, g.V),
        occ_levels, vir_levels,
    )
    return out, ladder


def body(rows, cols, amplitudes, integrals, fock_virtual, occ_levels, vir_levels, ladder_ints):
    g = sizes(rows, cols, amplitudes, ladder_ints)
    amps = jnp.transpose(amplitudes, (0, 2, 1, 3)).reshape(g.o, g.v * g.O, g.V)
    ints = jnp.transpose(integrals, (0, 2, 1, 3)).reshape(g.o, g.v * g.O, g.V)
    slab = ladder_ints.reshape(g.v * g.d, g.window, g.V)
    result, ladder = main_call(g, amps, ints, slab, fock_virtual, occ_levels, vir_levels)
    new_amps = jnp.transpose(result.reshape(g.o, g.v, g.O, g.V), (0, 2, 1, 3))
    ladder = ladder.reshape(g.window, g.O // rows, g.o, g.V)
    return (new_amps, jnp.transpose(ladder, (2, 1, 0, 3)).astype(BF16))


def solution(mesh):
    placed = (
        P("col", None, "row", None),
        P("col", None, "row", None),
        P(),
        P(),
        P(),
        P("row", "col", None, None),
    )
    return jax.shard_map(
        functools.partial(body, mesh.shape["row"], mesh.shape["col"]),
        mesh=mesh,
        in_specs=placed,
        out_specs=(P("col", None, "row", None), P("col", "row", None, None)),
        check_vma=False,
    )
```
